256 devices in a mesh: pool: 4 (over x_hi, core), frame: 16 (over x_lo, z), tensor: 4 (over y).
Axes of the slice: x: 4 (x_hi: 2, x_lo: 2; x = x_hi * 2 + x_lo), y: 4, z: 8, core: 2. Of those that a mesh axis runs over, the one named last changes fastest.
Arguments:
- latents: bfloat16 [32768, 2240], P(('pool', 'frame', 'tensor')), parts along dimension 0, may hold values from -6 to 6
- queries: bfloat16 [32768, 2240], P(('pool', 'frame'), 'tensor'), parts along dimension 0, may hold values from -6 to 6
- keys: bfloat16 [32768, 2240], P(('pool', 'frame'), 'tensor'), parts along dimension 0, may hold values from -6 to 6
- values: bfloat16 [32768, 2240], P(('pool', 'frame'), 'tensor'), parts along dimension 0, may hold values from -6 to 6
- log_decay: float32 [20, 32768], P('tensor', ('pool', 'frame')), parts along dimension 1, may hold values from -0.6 to 0, as said below
- block_ids: int32 [32768], P(('pool', 'frame')), parts along dimension 0, may hold values from 0 to 3, as said below
- t_index: int32 [4], P('pool'), parts along dimension 0, may hold values from 0 to 49
- w_mod: bfloat16 [256, 8960], replicated, may hold values from -0.375 to 0.375
- w_out: bfloat16 [2240, 2240], P('tensor', 'frame'), may hold values from -0.125 to 0.125
- w_up: bfloat16 [2240, 4480], P('frame', 'tensor'), may hold values from -0.125 to 0.125
- w_down: bfloat16 [4480, 2240], P('tensor', 'frame'), may hold values from -0.09375 to 0.09375
Outputs:
- velocity: bfloat16 [32768, 2240], P(('pool', 'frame', 'tensor')), parts along dimension 0
- advanced: bfloat16 [32768, 2240], P(('pool', 'frame', 'tensor')), parts along dimension 0
The draws below stay inside these ranges and needn't reach their ends.
There are 4 independent parts, one for each index of `pool`. The reference program is written for one: setup_inputs(seed, part) draws one part's arguments, and reference() takes and returns one part's arrays. A program takes and returns all parts, laid end to end along the dimension named above; an argument that names none is the same for every part. Nothing has to cross between parts.
Inputs may be any that keep to these rules, and one draw needn't show every extreme that they name: `block_ids`: within each span of 512 tokens the value never falls, starts at 0 and ends at 3. `log_decay`: every entry is negative.
All inputs are finite; a program needn't handle non-finite values.
Results may differ from the reference program's by a relative error of at most 0.0085.
Values may be sent and summed in bfloat16 or wider, within the bound.
No kernel may reach another device: no remote copies, remote signals or barrier semaphores. Data moves between devices by JAX's collectives and lax.ppermute only.
A program may use at most 128 MiB of HBM per device.

```python
import math
import jax
import jax.numpy as jnp
from jax import lax

D = 2240
ATTENTION_HEADS = 20
DH = 112
FFW = 4480
TEMB = 256
STEPS = 50
SUBS = 4
TOK_DEV = 512
SAMPLE_TOKENS = 8192
HD = 2240
N_FRAME = 16
N_TENSOR = 4


def draw_log_decay(key, part):
    random_subkeys = jax.random.split(key, 7)
    block_count = SAMPLE_TOKENS // TOK_DEV
    quick_share = 0.5
    quick_heads = jax.random.uniform(random_subkeys[0], (ATTENTION_HEADS, 1)) < quick_share
    quick_rate = jax.random.uniform(random_subkeys[1], (ATTENTION_HEADS, 1), minval=1.0 / 50.0, maxval=1.0 / 30.0)
    slow_rate = jax.random.uniform(random_subkeys[2], (ATTENTION_HEADS, 1), minval=0.1, maxval=0.3) / SAMPLE_TOKENS
    spread = jnp.exp(jax.random.uniform(random_subkeys[3], (ATTENTION_HEADS, block_count), minval=-math.log(2.0), maxval=math.log(2.0)))
    spread = jnp.repeat(spread, TOK_DEV, axis=1)
    roughness = jax.random.uniform(random_subkeys[4], (ATTENTION_HEADS, SAMPLE_TOKENS), minval=0.5, maxval=1.5)
    decay_speed = jnp.where(quick_heads, quick_rate, slow_rate) * spread * roughness
    spike_locations = jax.random.randint(random_subkeys[5], (3,), 0, SAMPLE_TOKENS)
    spike_mask = jnp.any(jnp.arange(SAMPLE_TOKENS)[None, :] == spike_locations[:, None], axis=0)
    spike_logarithm = jnp.log(jax.random.uniform(random_subkeys[6], (ATTENTION_HEADS, SAMPLE_TOKENS), minval=0.65, maxval=0.8))
    return (-decay_speed + jnp.where(spike_mask[None, :], spike_logarithm, 0.0)).astype(jnp.float32)


def draw_block_ids(key, part):
    block_count = SAMPLE_TOKENS // TOK_DEV
    cut_points = jax.random.randint(key, (block_count, 1, SUBS - 1), 1, TOK_DEV)
    places = jnp.arange(TOK_DEV).astype(jnp.int32)
    labels = jnp.sum((places[None, :, None] >= cut_points).astype(jnp.int32), axis=2)
    return labels.reshape(SAMPLE_TOKENS).astype(jnp.int32)


def levels(rng, extent, shards, least, top_value):
    level = 1.0
    for axis_at, shards_of in shards:
        heights = jax.random.uniform(jax.random.fold_in(jax.random.fold_in(rng, 6), axis_at), (shards_of,), jnp.float32, least / len(shards), top_value / len(shards))
        level = level * jnp.repeat(jnp.exp(heights), extent[axis_at] // shards_of).reshape((-1,) + (1,) * (len(extent) - 1 - axis_at))
    return level


def gaussian(rng, extent, deviation, bound, pieces=(), held_as=jnp.bfloat16):
    gain = levels(rng, extent, pieces, -0.22, 0.18) if pieces else 1.0
    values = jax.random.normal(rng, extent, jnp.float32) * deviation * gain
    return jnp.minimum(jnp.maximum(values, -bound), bound).astype(held_as)


def setup_inputs(seed: int = 0, part: int = 0) -> dict:
    arg_keys = jax.random.split(jax.random.key(seed), 12)
    own_keys = jax.random.split(jax.random.fold_in(arg_keys[11], part), 12)
    latents = gaussian(own_keys[0], (SAMPLE_TOKENS, D), 1.0, 6.0, ((0, 64),))
    queries = gaussian(own_keys[1], (SAMPLE_TOKENS, HD), 1.0, 6.0, ((0, 16), (1, 4)))
    keys = gaussian(own_keys[2], (SAMPLE_TOKENS, HD), 1.0, 6.0, ((0, 16), (1, 4)))
    values = gaussian(own_keys[3], (SAMPLE_TOKENS, HD), 1.0, 6.0, ((0, 16), (1, 4)))
    log_decay = draw_log_decay(jax.random.fold_in(jax.random.fold_in(arg_keys[11], part), 71), part)
    block_ids = draw_block_ids(jax.random.fold_in(jax.random.fold_in(arg_keys[11], part), 71), part)
    t_index = jax.random.randint(own_keys[6], (1,), 0, STEPS).astype(jnp.int32)
    w_mod = gaussian(arg_keys[7], (TEMB, 4 * D), TEMB ** -0.5, 0.375)
    w_out = gaussian(arg_keys[8], (HD, D), HD ** -0.5, 0.125, ((0, 4), (1, 16)))
    w_up = gaussian(arg_keys[9], (D, FFW), D ** -0.5, 0.125, ((0, 16), (1, 4)))
    w_down = gaussian(arg_keys[10], (FFW, D), FFW ** -0.5, 0.09375, ((0, 4), (1, 16)))
    return {"latents": latents, "queries": queries, "keys": keys, "values": values, "log_decay": log_decay, "block_ids": block_ids, "t_index": t_index, "w_mod": w_mod, "w_out": w_out, "w_up": w_up, "w_down": w_down}


def modulation_of(t_index, w_mod):
    fraction = 1.0 - t_index[0].astype(jnp.float32) / STEPS
    following = fraction - 1.0 / STEPS
    sigma_now = 3.0 * fraction / (1.0 + 2.0 * fraction)
    sigma_next = 3.0 * following / (1.0 + 2.0 * following)
    half_width = w_mod.shape[0] // 2
    frequency = jnp.exp(-math.log(10000.0) * jnp.arange(half_width).astype(jnp.float32) / half_width)
    angles = 1000.0 * sigma_now * frequency
    embedding = jnp.concatenate([jnp.cos(angles), jnp.sin(angles)])
    time_features = jax.nn.silu(embedding).astype(jnp.bfloat16)
    shifts = jnp.dot(time_features[None, :], w_mod, preferred_element_type=jnp.float32)[0]
    return (shifts, sigma_next - sigma_now)

def own_state(key_heads, value_heads, cumulative):
    block_total = cumulative[:, -1]
    scaled = key_heads.astype(jnp.float32) * jnp.exp(block_total[:, None] - cumulative)[:, :, None]
    state_sum = jnp.einsum('htd,hte->hde', scaled, value_heads.astype(jnp.float32), precision=lax.Precision.HIGHEST)
    return (block_total, state_sum)

def mix_block(query_heads, key_heads, value_heads, cumulative, labels, carried_state):
    factor = query_heads.shape[2] ** (-0.5)
    visible = labels[None, :] <= labels[:, None]
    decay = jnp.exp(jnp.minimum(cumulative[:, :, None] - cumulative[:, None, :], 0.0))
    weights = jnp.where(visible[None], decay, 0.0) * factor
    scores = jnp.einsum('hid,hjd->hij', query_heads.astype(jnp.float32), key_heads.astype(jnp.float32))
    probs = (scores * weights).astype(jnp.bfloat16)
    inner_part = jnp.einsum('hij,hjd->hid', probs.astype(jnp.float32), value_heads.astype(jnp.float32))
    carried = jnp.einsum('hid,hde->hie', query_heads.astype(jnp.float32), carried_state, precision=lax.Precision.HIGHEST)
    numerator = inner_part + carried * (jnp.exp(cumulative) * factor)[:, :, None]
    normed = numerator * lax.rsqrt(lax.optimization_barrier(jnp.mean(numerator * numerator, axis=2, keepdims=True)) + 1e-06)
    return normed.astype(jnp.bfloat16)

def layer_norm(hidden):
    centered = hidden - lax.optimization_barrier(jnp.mean(hidden, axis=1, keepdims=True))
    variance = lax.optimization_barrier(jnp.mean(centered * centered, axis=1, keepdims=True))
    return centered * lax.rsqrt(variance + 1e-06)

def reference(latents, queries, keys, values, log_decay, block_ids, t_index, w_mod, w_out, w_up, w_down):
    shifts, step_size = modulation_of(t_index, w_mod)
    width = latents.shape[1]
    query_blocks = queries.reshape(N_FRAME, TOK_DEV, ATTENTION_HEADS, DH).transpose(0, 2, 1, 3)
    key_blocks = keys.reshape(N_FRAME, TOK_DEV, ATTENTION_HEADS, DH).transpose(0, 2, 1, 3)
    value_blocks = values.reshape(N_FRAME, TOK_DEV, ATTENTION_HEADS, DH).transpose(0, 2, 1, 3)
    decay_blocks = log_decay.reshape(ATTENTION_HEADS, N_FRAME, TOK_DEV).transpose(1, 0, 2)
    label_blocks = block_ids.reshape(N_FRAME, TOK_DEV)

    def advance(carried_state, inputs):
        query_heads, key_heads, value_heads, decay_rows, labels = inputs
        cumulative = jnp.cumsum(decay_rows, axis=1)
        mixed = mix_block(query_heads, key_heads, value_heads, cumulative, labels, carried_state)
        block_total, state_sum = own_state(key_heads, value_heads, cumulative)
        following = jnp.exp(block_total)[:, None, None] * carried_state + state_sum
        return (following, mixed)
    initial = jnp.zeros((ATTENTION_HEADS, DH, DH), jnp.float32)
    final_state, mixed_blocks = lax.scan(advance, initial, (query_blocks, key_blocks, value_blocks, decay_blocks, label_blocks))
    heads_out = mixed_blocks.transpose(0, 2, 1, 3).reshape(SAMPLE_TOKENS, ATTENTION_HEADS * DH)
    group_heads = ATTENTION_HEADS * DH // N_TENSOR
    attention = jnp.zeros((SAMPLE_TOKENS, width), jnp.float32)
    for group in range(N_TENSOR):
        partial_sum = jnp.dot(heads_out[:, group * group_heads:(group + 1) * group_heads], w_out[group * group_heads:(group + 1) * group_heads], preferred_element_type=jnp.float32)
        attention = attention + lax.optimization_barrier(partial_sum.astype(jnp.bfloat16)).astype(jnp.float32)
    hidden = latents.astype(jnp.float32) + shifts[3 * width:] * attention
    normed = (layer_norm(hidden) * (1.0 + shifts[width:2 * width]) + shifts[:width]).astype(jnp.bfloat16)
    units = jax.nn.gelu(jnp.dot(normed, w_up, preferred_element_type=jnp.float32), approximate=True).astype(jnp.bfloat16)
    group_units = FFW // N_TENSOR
    feed = jnp.zeros((SAMPLE_TOKENS, width), jnp.float32)
    for group in range(N_TENSOR):
        partial_sum = jnp.dot(units[:, group * group_units:(group + 1) * group_units], w_down[group * group_units:(group + 1) * group_units], preferred_element_type=jnp.float32)
        feed = feed + lax.optimization_barrier(partial_sum.astype(jnp.bfloat16)).astype(jnp.float32)
    velocity = (hidden + shifts[2 * width:3 * width] * feed).astype(jnp.bfloat16)
    advanced = (latents.astype(jnp.float32) + step_size * velocity.astype(jnp.float32)).astype(jnp.bfloat16)
    return (velocity, advanced)
```

```python
import math

import jax
import jax.numpy as jnp
import numpy as np
from jax import lax
from jax.sharding import Mesh, PartitionSpec as P

STEPS = 50
BF = jnp.bfloat16
F32 = jnp.float32
AXES = {"xh": 2, "c": 2, "xl": 2, "z": 8, "y": 4}
PIECE = 70
PADDED = 72


def permute(block, axes, route):
    sizes = [AXES[a] for a in axes]
    pairs = []
    for i in range(int(np.prod(sizes))):
        target = route(*[int(v) for v in np.unravel_index(i, sizes)])
        if target is not None:
            pairs.append((i, int(np.ravel_multi_index(target, sizes))))
    return lax.ppermute(block, tuple(axes) if len(axes) > 1 else axes[0], pairs)


def along_y(block, d):
    return permute(block, ("y",), lambda y: ((y + d) % 4,))


def along_z(block, d):
    return permute(block, ("z",), lambda z: ((z + d) % 8,))


def along_x(block, d):
    def route(xh, xl):
        x = (2 * xh + xl + d) % 4
        return (x // 2, x % 2)

    return permute(block, ("xh", "xl"), route)


def along_frame(block, d):
    def route(xl, z):
        f = 8 * xl + z + d
        return (f // 8, f % 8) if f < 16 else None

    return permute(block, ("xl", "z"), route)


def other_core(block):
    return permute(block, ("c",), lambda c: (1 - c,))


def modulation_of(t_index, w_mod):
    fraction = 1.0 - t_index[0].astype(F32) / STEPS
    following = fraction - 1.0 / STEPS
    sigma_now = 3.0 * fraction / (1.0 + 2.0 * fraction)
    sigma_next = 3.0 * following / (1.0 + 2.0 * following)
    half_width = w_mod.shape[0] // 2
    frequency = jnp.exp(-math.log(10000.0) * jnp.arange(half_width).astype(F32) / half_width)
    angles = 1000.0 * sigma_now * frequency
    embedding = jnp.concatenate([jnp.cos(angles), jnp.sin(angles)])
    time_features = jax.nn.silu(embedding).astype(BF)
    shifts = jnp.dot(time_features[None, :], w_mod, preferred_element_type=F32)[0]
    return (shifts, sigma_next - sigma_now)


Z_ORDER = (0, -1, -2, -3, -4, 1, 2, 3)


def piece_order():
    c, xl, z = lax.axis_index("c"), lax.axis_index("xl"), lax.axis_index("z")
    order = []
    for h in range(2):
        for x in range(2):
            for d in Z_ORDER:
                f = jnp.where(x == 0, xl, 1 - xl) * 8 + (z + d + 8) % 8
                order.append(2 * f + jnp.where(h == 0, c, 1 - c))
    return jnp.stack(order).astype(jnp.int32)


def halves(rows):
    both = jnp.pad(rows.reshape(2, PIECE, rows.shape[1]), ((0, 0), (0, PADDED - PIECE), (0, 0)))
    return jnp.where(lax.axis_index("c") == 0, both[0], both[1])


def z_ring(block):
    up, down = [block], [block]
    for _ in range(4):
        up.append(along_z(up[-1], 1))
    for _ in range(3):
        down.append(along_z(down[-1], -1))
    return up[1:], down[1:]


def gather_out(w_out):
    mine = halves(w_out.T)
    pair = jnp.stack([mine, along_x(mine, 1)])
    up, down = z_ring(pair)
    every = jnp.stack([pair] + up + down, axis=1)
    return jnp.concatenate([every, other_core(every)]).reshape(32 * PADDED, -1)


def gather_ffn(w_up, w_down):
    mine = jnp.stack([halves(w_up), halves(w_down.T)])
    up, down = z_ring(mine)
    first = jnp.stack([mine] + up[:3], axis=1)
    second = jnp.stack([up[3]] + down, axis=1)
    first_x = along_x(first, 1)
    second_x = along_x(second, -1)
    every = jnp.concatenate([first, second, first_x, second_x], axis=1)
    other = other_core(every)
    both = jnp.concatenate([every, other], axis=1)
    both = both.reshape(2, 32 * PADDED, -1)
    return both[0], both[1]


def packed_state(state, total):
    hi = total.astype(BF)
    mid = (total - hi.astype(F32)).astype(BF)
    low = (total - hi.astype(F32) - mid.astype(F32)).astype(BF)
    parts = jnp.stack([hi, mid, low] + [jnp.zeros_like(hi)] * 13, axis=1)
    return jnp.concatenate(
        [state.astype(BF), jnp.broadcast_to(parts[:, None, :], (5, 112, 16))], axis=2
    )


def unpacked_state(packed):
    parts = packed[:, 0, 112:115].astype(F32)
    return packed[:, :, :112].astype(F32), parts[:, 0] + parts[:, 1] + parts[:, 2]


def chained(blocks):
    state, total = blocks[-1]
    for s, t in blocks[-2::-1]:
        state = s + jnp.exp(t)[:, None, None] * state
        total = total + t
    return state, total


def earlier_state(state, total):
    sent = packed_state(state, total)
    near = [unpacked_state(along_frame(sent, d)) for d in (1, 2, 3)]
    group = packed_state(*chained([(state, total)] + near))
    far = [unpacked_state(along_frame(group, d)) for d in (1, 5, 9, 13)]
    return chained(far)[0]


def on_device(
    latents, queries, keys, values, log_decay, block_ids, t_index, w_mod, w_out, w_up, w_down
):
    width = latents.shape[1]
    head_count, token_count = log_decay.shape
    head_size = queries.shape[1] // head_count
    share = token_count // 4
    y = lax.axis_index("y")

    def to_heads(rows_in):
        return rows_in.T.reshape(head_count, head_size, token_count)

    query_heads, key_heads, value_heads = to_heads(queries), to_heads(keys), to_heads(values)
    cumulative = jnp.cumsum(log_decay, axis=1)
    total = cumulative[:, -1]
    scaled = (key_heads.astype(F32) * jnp.exp(total[:, None] - cumulative)[:, None, :]).astype(BF)
    state = jnp.einsum("hdt,het->hde", scaled, value_heads, preferred_element_type=F32)

    out_weight = gather_out(w_out)
    before = earlier_state(state, total)
    up_weight, down_weight = gather_ffn(w_up, w_down)

    factor = head_size ** (-0.5)
    visible = block_ids[None, :] <= block_ids[:, None]
    decay = jnp.exp(jnp.minimum(cumulative[:, :, None] - cumulative[:, None, :], 0.0))
    weights = jnp.where(visible[None], decay, 0.0) * factor
    scores = jnp.einsum("hdi,hdj->hij", query_heads, key_heads, preferred_element_type=F32)
    probs = (scores * weights).astype(BF)
    inner = jnp.einsum("hdj,hij->hdi", value_heads, probs, preferred_element_type=F32)
    carried = jnp.einsum("hde,hdi->hei", before.astype(BF), query_heads, preferred_element_type=F32)
    numerator = inner + carried * (jnp.exp(cumulative) * factor)[:, None, :]
    mixed = numerator * lax.rsqrt(jnp.mean(numerator * numerator, axis=1, keepdims=True) + 1e-06)
    mixed = mixed.astype(BF).reshape(head_count * head_size, token_count)

    def tokens_of(block, d):
        return lax.dynamic_slice_in_dim(block, ((y + d) % 4) * share, share, axis=1)

    def head_terms(d):
        return jnp.dot(out_weight, tokens_of(mixed, d), preferred_element_type=F32).astype(BF)

    terms = [along_y(head_terms(d), d) for d in (2, 1, 3)] + [head_terms(0)]
    attention = sum(t.astype(F32) for t in terms)

    shifts, step_size = modulation_of(t_index, w_mod)
    order = piece_order()

    def own_order(natural):
        pieces = jnp.pad(
            natural.reshape(32, PIECE, -1), ((0, 0), (0, PADDED - PIECE), (0, 0))
        )
        return jnp.take(pieces, order, axis=0).reshape(32 * PADDED, -1)

    vectors = own_order(shifts.reshape(4, width).T)
    shift, scale, ffn_gate, attention_gate = [vectors[:, i : i + 1] for i in range(4)]
    latent = own_order(latents.T).astype(F32)
    real = (jnp.arange(32 * PADDED) % PADDED < PIECE)[:, None]
    hidden = latent + attention_gate * attention
    mean = jnp.sum(hidden, axis=0, keepdims=True) / width
    centered = jnp.where(real, hidden - mean, 0.0)
    variance = jnp.sum(centered * centered, axis=0, keepdims=True) / width
    normed = (centered * lax.rsqrt(variance + 1e-06) * (1.0 + scale) + shift).astype(BF)

    def unit_terms(tokens):
        sums = lax.dot_general(
            up_weight, tokens, (((0,), (0,)), ((), ())), preferred_element_type=F32
        )
        units = jax.nn.gelu(sums, approximate=True).astype(BF)
        return jnp.dot(down_weight, units, preferred_element_type=F32).astype(BF)

    theirs = {d: along_y(normed, -d) for d in (1, 3, 2)}
    feeds = [unit_terms(normed)] + [along_y(unit_terms(theirs[d]), d) for d in (1, 3, 2)]
    feed = sum(t.astype(F32) for t in feeds)
    velocity = (hidden + ffn_gate * feed).astype(BF)
    advanced = (latent + step_size * velocity.astype(F32)).astype(BF)
    back = jnp.zeros((32,), jnp.int32).at[order].set(jnp.arange(32, dtype=jnp.int32))

    def natural_order(own):
        pieces = jnp.take(own.reshape(32, PADDED, share), back, axis=0)
        return pieces[:, :PIECE].reshape(width, share).T

    return (natural_order(velocity), natural_order(advanced))


def solution(mesh):
    fine = Mesh(mesh.devices.reshape(tuple(AXES.values())), tuple(AXES))
    pool, frame = ("xh", "c"), ("xl", "z")
    rows = P(pool + frame + ("y",), None)
    return jax.shard_map(
        on_device,
        mesh=fine,
        in_specs=(
            rows,
            P(pool + frame, "y"),
            P(pool + frame, "y"),
            P(pool + frame, "y"),
            P("y", pool + frame),
            P(pool + frame),
            P(pool),
            P(),
            P("y", frame),
            P(frame, "y"),
            P("y", frame),
        ),
        out_specs=(rows, rows),
        check_vma=False,
    )
```

```python
import functools
import math

import jax
import jax.numpy as jnp
import numpy as np
from jax import lax
from jax.experimental import pallas as pl
from jax.experimental.pallas import tpu as pltpu
from jax.sharding import Mesh, PartitionSpec as P

STEPS = 50
BF = jnp.bfloat16
F32 = jnp.float32
AXES = {"xh": 2, "c": 2, "xl": 2, "z": 8, "y": 4}
HEADS = 5
DH = 112
TOKENS = 512
SHARE = 128
WIDTH = 2240
PIECE = 70
PADDED = 72
PIECES = 32
ROWS = PIECES * PADDED
VMEM = pl.BlockSpec(memory_space=pltpu.VMEM)
SMEM = pl.BlockSpec(memory_space=pltpu.SMEM)


def permute(block, axes, route):
    sizes = [AXES[a] for a in axes]
    pairs = []
    for i in range(int(np.prod(sizes))):
        target = route(*[int(v) for v in np.unravel_index(i, sizes)])
        if target is not None:
            pairs.append((i, int(np.ravel_multi_index(target, sizes))))
    return lax.ppermute(block, tuple(axes) if len(axes) > 1 else axes[0], pairs)


def along_y(block, d):
    return permute(block, ("y",), lambda y: ((y + d) % 4,))


def along_x(block, d):
    def route(xh, xl):
        x = (2 * xh + xl + d) % 4
        return (x // 2, x % 2)

    return permute(block, ("xh", "xl"), route)


def along_frame(block, d):
    def route(xl, z):
        f = 8 * xl + z + d
        return (f // 8, f % 8) if f < 16 else None

    return permute(block, ("xl", "z"), route)


def other_core(block):
    return permute(block, ("c",), lambda c: (1 - c,))


def cost(flops, size):
    return pl.CostEstimate(flops=flops, bytes_accessed=size, transcendentals=0)


def modulation_of(t_index, w_mod):
    fraction = 1.0 - t_index[0].astype(F32) / STEPS
    following = fraction - 1.0 / STEPS
    sigma_now = 3.0 * fraction / (1.0 + 2.0 * fraction)
    sigma_next = 3.0 * following / (1.0 + 2.0 * following)
    half_width = w_mod.shape[0] // 2
    frequency = jnp.exp(-math.log(10000.0) * jnp.arange(half_width).astype(F32) / half_width)
    angles = 1000.0 * sigma_now * frequency
    embedding = jnp.concatenate([jnp.cos(angles), jnp.sin(angles)])
    time_features = jax.nn.silu(embedding).astype(BF)
    shifts = jnp.dot(time_features[None, :], w_mod, preferred_element_type=F32)[0]
    return (lax.optimization_barrier(shifts), sigma_next - sigma_now)


def padded_pieces(rows):
    pieces = rows.reshape(-1, PIECE, rows.shape[1])
    return jnp.pad(pieces, ((0, 0), (0, PADDED - PIECE), (0, 0)))


def total_lanes(total):
    hi = total.astype(BF).astype(F32)
    mid = (total - hi).astype(BF).astype(F32)
    low = total - hi - mid
    lane = lax.broadcasted_iota(jnp.int32, (DH, 16), 1)
    zero = jnp.zeros((DH, 16), F32)
    return jnp.where(lane == 0, hi, jnp.where(lane == 1, mid, jnp.where(lane == 2, low, zero))).astype(BF)


def state_kernel(k_ref, v_ref, decay_ref, cumulative_ref, packed_ref):
    decay = decay_ref[...]
    hi = decay.astype(BF)
    rest = decay - hi.astype(F32)
    mid = rest.astype(BF)
    low = (rest - mid.astype(F32)).astype(BF)
    row = lax.broadcasted_iota(jnp.int32, (TOKENS, TOKENS), 0)
    column = lax.broadcasted_iota(jnp.int32, (TOKENS, TOKENS), 1)
    triangle = jnp.where(row <= column, 1.0, 0.0).astype(BF)
    cumulative = sum(
        jnp.dot(part, triangle, preferred_element_type=F32) for part in (low, mid, hi)
    )
    cumulative_ref[...] = cumulative
    for h in range(HEADS):
        mine = cumulative[h : h + 1, :]
        total = mine[:, TOKENS - 1 :]
        heads = pl.ds(DH * h, DH)
        scaled = (k_ref[heads, :].astype(F32) * jnp.exp(total - mine)).astype(BF)
        state = lax.dot_general(
            v_ref[heads, :], scaled, (((1,), (1,)), ((), ())), preferred_element_type=F32
        )
        packed_ref[h, :, 0:DH] = state.astype(BF)
        packed_ref[h, :, DH:SHARE] = total_lanes(total)


def own_state(keys, values, log_decay):
    return pl.pallas_call(
        state_kernel,
        out_shape=(
            jax.ShapeDtypeStruct((HEADS, TOKENS), F32),
            jax.ShapeDtypeStruct((HEADS, DH, SHARE), BF),
        ),
        in_specs=[VMEM] * 3,
        out_specs=(VMEM, VMEM),
        cost_estimate=cost(10**9, 3 * 10**6),
    )(keys, values, log_decay)


def chained(refs, h):
    state = total = None
    for ref in reversed(refs):
        packed = ref[h].astype(F32)
        mine = jnp.sum(packed[0:1, DH : DH + 3], axis=1, keepdims=True)
        state = packed if state is None else packed + jnp.exp(mine) * state
        total = mine if total is None else total + mine
    return state, total


def chain_kernel(a_ref, b_ref, c_ref, d_ref, out_ref):
    for h in range(HEADS):
        state, total = chained([a_ref, b_ref, c_ref, d_ref], h)
        out_ref[h] = state.astype(BF)
        out_ref[h, :, DH:SHARE] = total_lanes(total)


def chain(blocks):
    return pl.pallas_call(
        chain_kernel,
        out_shape=jax.ShapeDtypeStruct((HEADS, DH, SHARE), BF),
        in_specs=[VMEM] * 4,
        out_specs=VMEM,
        cost_estimate=cost(10**6, 10**6),
    )(*blocks)


def inner_kernel(q_ref, k_ref, v_ref, cumulative_ref, labels_ref, out_ref):
    cumulative = cumulative_ref[...]
    labels = labels_ref[...].astype(F32)
    stacked = jnp.concatenate([cumulative, labels, jnp.zeros((2, TOKENS), F32)], axis=0)
    columns = stacked.T
    visible = columns[:, HEADS : HEADS + 1] <= labels
    for h in range(HEADS):
        heads = pl.ds(DH * h, DH)
        scores = lax.dot_general(
            k_ref[heads, :], q_ref[heads, :], (((0,), (0,)), ((), ())), preferred_element_type=F32
        )
        decay = jnp.exp(jnp.minimum(cumulative[h : h + 1, :] - columns[:, h : h + 1], 0.0))
        weights = jnp.where(visible, decay * (DH**-0.5), 0.0)
        probs = (scores * weights).astype(BF)
        out_ref[heads, :] = jnp.dot(v_ref[heads, :], probs, preferred_element_type=F32)


def inner_part(queries, keys, values, cumulative, labels):
    return pl.pallas_call(
        inner_kernel,
        out_shape=jax.ShapeDtypeStruct((HEADS * DH, TOKENS), F32),
        in_specs=[VMEM] * 5,
        out_specs=VMEM,
        cost_estimate=cost(5 * 10**9, 4 * 10**6),
    )(queries, keys, values, cumulative, labels)


def mix_kernel(q_ref, inner_ref, cumulative_ref, a_ref, b_ref, c_ref, d_ref, out_ref):
    for h in range(HEADS):
        state, _ = chained([a_ref, b_ref, c_ref, d_ref], h)
        heads = pl.ds(DH * h, DH)
        carried = jnp.dot(state[:, 0:DH].astype(BF), q_ref[heads, :], preferred_element_type=F32)
        numerator = inner_ref[heads, :] + carried * (
            jnp.exp(cumulative_ref[h : h + 1, :]) * (DH**-0.5)
        )
        mean = jnp.sum(numerator * numerator, axis=0, keepdims=True) * (1.0 / DH)
        out_ref[heads, :] = (numerator * lax.rsqrt(mean + 1e-06)).astype(BF)


def mix(queries, inner, cumulative, far):
    return pl.pallas_call(
        mix_kernel,
        out_shape=jax.ShapeDtypeStruct((HEADS * DH, TOKENS), BF),
        in_specs=[VMEM] * 7,
        out_specs=VMEM,
        cost_estimate=cost(10**8, 4 * 10**6),
    )(queries, inner, cumulative, *far)


def piece_table(place_ref):
    c, xl = place_ref[0], place_ref[1]
    for hr in range(2):
        for z in range(8):
            for xr in range(2):
                h = c if hr == 0 else 1 - c
                x = xl if xr == 0 else 1 - xl
                yield hr * 16 + z * 2 + xr, 2 * (8 * x + z) + h, 4 * z + 2 * xr + h


def norm_kernel(place_ref, t0, t1, t2, t3, latent_ref, vector_ref, hidden_ref, normed_ref, work):
    sums = jnp.zeros((PADDED, SHARE), F32)
    for own, natural, term in piece_table(place_ref):
        attention = sum(t[term].astype(F32) for t in (t0, t1, t2, t3))
        hidden = latent_ref[natural].astype(F32) + vector_ref[natural][:, 3:4] * attention
        hidden_ref[own] = hidden
        sums = sums + hidden
    mean = jnp.sum(sums, axis=0, keepdims=True) * (1.0 / WIDTH)
    real = lax.broadcasted_iota(jnp.int32, (PADDED, SHARE), 0) < PIECE
    squares = jnp.zeros((PADDED, SHARE), F32)
    for own in range(PIECES):
        centered = hidden_ref[own] - mean
        squares = squares + centered * centered
    squares = jnp.where(real, squares, 0.0)
    scaling = lax.rsqrt(jnp.sum(squares, axis=0, keepdims=True) * (1.0 / WIDTH) + 1e-06)
    for own, natural, _ in piece_table(place_ref):
        vectors = vector_ref[natural]
        normed = (hidden_ref[own] - mean) * scaling * (1.0 + vectors[:, 1:2]) + vectors[:, 0:1]
        work[own * PADDED : (own + 1) * PADDED, :] = jnp.where(real, normed, 0.0)
    for i in range(ROWS // 256):
        normed_ref[:, 256 * i : 256 * (i + 1)] = work[256 * i : 256 * (i + 1), :].T.astype(BF)


def norm(place, terms, latents, vectors):
    return pl.pallas_call(
        norm_kernel,
        out_shape=(
            jax.ShapeDtypeStruct((PIECES, PADDED, SHARE), F32),
            jax.ShapeDtypeStruct((SHARE, ROWS), BF),
        ),
        in_specs=[SMEM] + [VMEM] * 6,
        out_specs=(VMEM, VMEM),
        scratch_shapes=[pltpu.VMEM((ROWS, SHARE), F32)],
        cost_estimate=cost(10**7, 8 * 10**6),
    )(place, *[t.reshape(PIECES, PADDED, SHARE) for t in terms], latents, vectors)


def last_kernel(place_ref, step_ref, f0, f1, f2, f3, hidden_ref, latent_ref, vector_ref, v_ref, a_ref):
    step = step_ref[0]
    for own, natural, _ in piece_table(place_ref):
        feed = sum(f[own].astype(F32) for f in (f0, f1, f2, f3))
        velocity = (hidden_ref[own] + vector_ref[natural][:, 2:3] * feed).astype(BF)
        v_ref[natural] = velocity
        a_ref[natural] = (latent_ref[natural].astype(F32) + step * velocity.astype(F32)).astype(BF)


def last(place, step_size, feeds, hidden, latents, vectors):
    shape = jax.ShapeDtypeStruct((PIECES, PADDED, SHARE), BF)
    return pl.pallas_call(
        last_kernel,
        out_shape=(shape, shape),
        in_specs=[SMEM] * 2 + [VMEM] * 7,
        out_specs=(VMEM, VMEM),
        cost_estimate=cost(10**7, 8 * 10**6),
    )(place, step_size, *[f.reshape(PIECES, PADDED, SHARE) for f in feeds], hidden, latents, vectors)


BLOCK = 384
HALF = ROWS // 2
PER_HALF = HALF // BLOCK
UP_STEPS = 2 * PER_HALF


def units_kernel(chunks, *refs):
    token_refs = refs[:chunks]
    up0, up1, down0, down1, out_ref, sums, units = refs[chunks:]
    step = pl.program_id(0)

    @pl.when(step == 0)
    def _():
        sums[...] = jnp.zeros_like(sums)

    def up(weight):
        columns = pl.ds(pl.multiple_of(step * BLOCK, BLOCK), BLOCK)
        for n, token_ref in enumerate(token_refs):
            rows = pl.ds(SHARE * n, SHARE)
            sums[rows, :] += jnp.dot(token_ref[:, columns], weight[...], preferred_element_type=F32)

    @pl.when(step < PER_HALF)
    def _():
        up(up0)

    @pl.when((step >= PER_HALF) & (step < UP_STEPS))
    def _():
        up(up1)

    @pl.when(step == UP_STEPS - 1)
    def _():
        units[...] = jax.nn.gelu(sums[...], approximate=True).astype(BF)

    def down(weight):
        feed = lax.dot_general(
            weight[...], units[...], (((1,), (1,)), ((), ())), preferred_element_type=F32
        ).astype(BF)
        for n in range(chunks):
            out_ref[n] = feed[:, SHARE * n : SHARE * (n + 1)]

    @pl.when((step >= UP_STEPS) & (step < UP_STEPS + PER_HALF))
    def _():
        down(down0)

    @pl.when(step >= UP_STEPS + PER_HALF)
    def _():
        down(down1)


def unit_terms(tokens, weights):
    chunks = len(tokens)
    hidden_units = weights[0].shape[1]

    def block(first):
        return pl.BlockSpec(
            (BLOCK, hidden_units), lambda i: (jnp.clip(i - first, 0, PER_HALF - 1), 0)
        )

    out = pl.pallas_call(
        functools.partial(units_kernel, chunks),
        grid=(2 * UP_STEPS,),
        out_shape=jax.ShapeDtypeStruct((chunks, ROWS, SHARE), BF),
        in_specs=[pl.BlockSpec((SHARE, ROWS), lambda i: (0, 0))] * chunks
        + [block(PER_HALF * k) for k in range(4)],
        out_specs=pl.BlockSpec(
            (chunks, BLOCK, SHARE), lambda i: (0, jnp.maximum(i - UP_STEPS, 0), 0)
        ),
        scratch_shapes=[
            pltpu.VMEM((SHARE * chunks, hidden_units), F32),
            pltpu.VMEM((SHARE * chunks, hidden_units), BF),
        ],
        cost_estimate=cost(
            4 * SHARE * chunks * ROWS * hidden_units, 4 * ROWS * hidden_units
        ),
    )(*tokens, *weights)
    return [out[n] for n in range(chunks)]


def on_device(
    latents, queries, keys, values, log_decay, block_ids, t_index, w_mod, w_out, w_up, w_down
):
    y, c, xl = lax.axis_index("y"), lax.axis_index("c"), lax.axis_index("xl")
    place = jnp.stack([c, xl]).astype(jnp.int32)

    out_mine = padded_pieces(w_out.T).reshape(2 * PADDED, -1)
    out_pair = jnp.stack([out_mine, along_x(out_mine, 1)])
    out_weight = lax.all_gather(out_pair, "z", axis=0).reshape(ROWS, -1)
    both = jnp.stack([padded_pieces(w_up), padded_pieces(w_down.T)])
    mine = jnp.where(c == 0, both[:, 0], both[:, 1])
    pair = jnp.stack([mine, along_x(mine, 1)], axis=1)
    up_half = lax.all_gather(pair[0], "z", axis=0).reshape(HALF, -1)
    down_half = lax.all_gather(pair[1], "z", axis=0).reshape(HALF, -1)

    queries, keys, values = queries.T, keys.T, values.T
    cumulative, packed = own_state(keys, values, log_decay)
    group = chain([packed] + [along_frame(packed, d) for d in (1, 2, 3)])
    far = [along_frame(group, d) for d in (1, 5, 9, 13)]
    inner = inner_part(queries, keys, values, cumulative, block_ids[None, :])
    mixed = mix(queries, inner, cumulative, far)

    def head_terms(d):
        tokens = lax.dynamic_slice_in_dim(mixed, ((y + d) % 4) * SHARE, SHARE, axis=1)
        return jnp.dot(out_weight, tokens, preferred_element_type=F32).astype(BF)

    terms = [along_y(head_terms(d), d) for d in (2, 1, 3)] + [head_terms(0)]

    shifts, step_size = modulation_of(t_index, w_mod)
    vectors = padded_pieces(shifts.reshape(4, WIDTH).T)
    latent_pieces = padded_pieces(latents.T)
    hidden, normed = norm(place, terms, latent_pieces, vectors)

    theirs = {d: along_y(normed, -d) for d in (1, 3, 2)}
    weights = [up_half, other_core(up_half), down_half, other_core(down_half)]
    near = unit_terms([theirs[1], theirs[3]], weights)
    feeds = [along_y(near[0], 1), along_y(near[1], 3)]
    rest = unit_terms([normed, theirs[2]], weights)
    feeds += [rest[0], along_y(rest[1], 2)]
    step = step_size[None] if step_size.ndim == 0 else step_size
    velocity, advanced = last(place, step, feeds, hidden, latent_pieces, vectors)

    def natural(pieces):
        return pieces[:, :PIECE].reshape(WIDTH, SHARE).T

    return (natural(velocity), natural(advanced))


def solution(mesh):
    fine = Mesh(mesh.devices.reshape(tuple(AXES.values())), tuple(AXES))
    pool, frame = ("xh", "c"), ("xl", "z")
    rows = P(pool + frame + ("y",), None)
    return jax.shard_map(
        on_device,
        mesh=fine,
        in_specs=(
            rows,
            P(pool + frame, "y"),
            P(pool + frame, "y"),
            P(pool + frame, "y"),
            P("y", pool + frame),
            P(pool + frame),
            P(pool),
            P(),
            P("y", frame),
            P(frame, "y"),
            P("y", frame),
        ),
        out_specs=(rows, rows),
        check_vma=False,
    )
```

```python
import functools
import math

import jax
import jax.numpy as jnp
import numpy as np
from jax import lax
from jax.experimental import pallas as pl
from jax.experimental.pallas import tpu as pltpu
from jax.sharding import Mesh, PartitionSpec as P

STEPS = 50
BF = jnp.bfloat16
F32 = jnp.float32
AXES = {"xh": 2, "c": 2, "xl": 2, "z": 8, "y": 4}
HEADS = 5
DH = 112
TOKENS = 512
SHARE = 128
WIDTH = 2240
PIECE = 70
PADDED = 72
PIECES = 32
ROWS = PIECES * PADDED
VMEM = pl.BlockSpec(memory_space=pltpu.VMEM)
SMEM = pl.BlockSpec(memory_space=pltpu.SMEM)


def permute(block, axes, route):
    sizes = [AXES[a] for a in axes]
    pairs = []
    for i in range(int(np.prod(sizes))):
        target = route(*[int(v) for v in np.unravel_index(i, sizes)])
        if target is not None:
            pairs.append((i, int(np.ravel_multi_index(target, sizes))))
    return lax.ppermute(block, tuple(axes) if len(axes) > 1 else axes[0], pairs)


def along_y(block, d):
    return permute(block, ("y",), lambda y: ((y + d) % 4,))


def along_x(block, d):
    def route(xh, xl):
        x = (2 * xh + xl + d) % 4
        return (x // 2, x % 2)

    return permute(block, ("xh", "xl"), route)


def along_frame(block, d):
    def route(xl, z):
        f = 8 * xl + z + d
        return (f // 8, f % 8) if f < 16 else None

    return permute(block, ("xl", "z"), route)


def other_core(block):
    return permute(block, ("c",), lambda c: (1 - c,))


def in_vmem(block):
    return pltpu.with_memory_space_constraint(block, pltpu.VMEM)


def cost(flops, size):
    return pl.CostEstimate(flops=flops, bytes_accessed=size, transcendentals=0)


def modulation_of(t_index, w_mod):
    fraction = 1.0 - t_index[0].astype(F32) / STEPS
    following = fraction - 1.0 / STEPS
    sigma_now = 3.0 * fraction / (1.0 + 2.0 * fraction)
    sigma_next = 3.0 * following / (1.0 + 2.0 * following)
    half_width = w_mod.shape[0] // 2
    frequency = jnp.exp(-math.log(10000.0) * jnp.arange(half_width).astype(F32) / half_width)
    angles = 1000.0 * sigma_now * frequency
    embedding = jnp.concatenate([jnp.cos(angles), jnp.sin(angles)])
    time_features = jax.nn.silu(embedding).astype(BF)
    shifts = jnp.dot(time_features[None, :], w_mod, preferred_element_type=F32)[0]
    return (lax.optimization_barrier(shifts), sigma_next - sigma_now)


def padded_pieces(rows):
    pieces = rows.reshape(-1, PIECE, rows.shape[1])
    return jnp.pad(pieces, ((0, 0), (0, PADDED - PIECE), (0, 0)))


def total_lanes(total):
    hi = total.astype(BF).astype(F32)
    mid = (total - hi).astype(BF).astype(F32)
    low = total - hi - mid
    lane = lax.broadcasted_iota(jnp.int32, (DH, 16), 1)
    zero = jnp.zeros((DH, 16), F32)
    return jnp.where(lane == 0, hi, jnp.where(lane == 1, mid, jnp.where(lane == 2, low, zero))).astype(BF)


def state_kernel(k_ref, v_ref, decay_ref, cumulative_ref, packed_ref):
    decay = decay_ref[...]
    hi = decay.astype(BF)
    rest = decay - hi.astype(F32)
    mid = rest.astype(BF)
    low = (rest - mid.astype(F32)).astype(BF)
    row = lax.broadcasted_iota(jnp.int32, (TOKENS, TOKENS), 0)
    column = lax.broadcasted_iota(jnp.int32, (TOKENS, TOKENS), 1)
    triangle = jnp.where(row <= column, 1.0, 0.0).astype(BF)
    cumulative = sum(
        jnp.dot(part, triangle, preferred_element_type=F32) for part in (low, mid, hi)
    )
    cumulative_ref[...] = cumulative
    for h in range(HEADS):
        mine = cumulative[h : h + 1, :]
        total = mine[:, TOKENS - 1 :]
        heads = pl.ds(DH * h, DH)
        scaled = (k_ref[heads, :].astype(F32) * jnp.exp(total - mine)).astype(BF)
        state = lax.dot_general(
            v_ref[heads, :], scaled, (((1,), (1,)), ((), ())), preferred_element_type=F32
        )
        packed_ref[h, :, 0:DH] = state.astype(BF)
        packed_ref[h, :, DH:SHARE] = total_lanes(total)


def own_state(keys, values, log_decay):
    return pl.pallas_call(
        state_kernel,
        out_shape=(
            jax.ShapeDtypeStruct((HEADS, TOKENS), F32),
            jax.ShapeDtypeStruct((HEADS, DH, SHARE), BF),
        ),
        in_specs=[VMEM] * 3,
        out_specs=(VMEM, VMEM),
        cost_estimate=cost(10**9, 3 * 10**6),
    )(keys, values, log_decay)


def chained(refs, h):
    state = total = None
    for ref in reversed(refs):
        packed = ref[h].astype(F32)
        mine = jnp.sum(packed[0:1, DH : DH + 3], axis=1, keepdims=True)
        state = packed if state is None else packed + jnp.exp(mine) * state
        total = mine if total is None else total + mine
    return state, total


def chain_kernel(a_ref, b_ref, c_ref, d_ref, out_ref):
    for h in range(HEADS):
        state, total = chained([a_ref, b_ref, c_ref, d_ref], h)
        out_ref[h] = state.astype(BF)
        out_ref[h, :, DH:SHARE] = total_lanes(total)


def chain(blocks):
    return pl.pallas_call(
        chain_kernel,
        out_shape=jax.ShapeDtypeStruct((HEADS, DH, SHARE), BF),
        in_specs=[VMEM] * 4,
        out_specs=VMEM,
        cost_estimate=cost(10**6, 10**6),
    )(*[in_vmem(b) for b in blocks])


def inner_kernel(q_ref, k_ref, v_ref, cumulative_ref, labels_ref, out_ref):
    cumulative = cumulative_ref[...]
    labels = labels_ref[...].astype(F32)
    stacked = jnp.concatenate([cumulative, labels, jnp.zeros((2, TOKENS), F32)], axis=0)
    columns = stacked.T
    visible = columns[:, HEADS : HEADS + 1] <= labels
    for h in range(HEADS):
        heads = pl.ds(DH * h, DH)
        scores = lax.dot_general(
            k_ref[heads, :], q_ref[heads, :], (((0,), (0,)), ((), ())), preferred_element_type=F32
        )
        decay = jnp.exp(jnp.minimum(cumulative[h : h + 1, :] - columns[:, h : h + 1], 0.0))
        weights = jnp.where(visible, decay * (DH**-0.5), 0.0)
        probs = (scores * weights).astype(BF)
        out_ref[heads, :] = jnp.dot(v_ref[heads, :], probs, preferred_element_type=F32)


def inner_part(queries, keys, values, cumulative, labels):
    return pl.pallas_call(
        inner_kernel,
        out_shape=jax.ShapeDtypeStruct((HEADS * DH, TOKENS), F32),
        in_specs=[VMEM] * 5,
        out_specs=VMEM,
        cost_estimate=cost(5 * 10**9, 4 * 10**6),
    )(queries, keys, values, cumulative, labels)


def mix_kernel(q_ref, inner_ref, cumulative_ref, a_ref, b_ref, c_ref, d_ref, out_ref):
    for h in range(HEADS):
        state, _ = chained([a_ref, b_ref, c_ref, d_ref], h)
        heads = pl.ds(DH * h, DH)
        carried = jnp.dot(state[:, 0:DH].astype(BF), q_ref[heads, :], preferred_element_type=F32)
        numerator = inner_ref[heads, :] + carried * (
            jnp.exp(cumulative_ref[h : h + 1, :]) * (DH**-0.5)
        )
        mean = jnp.sum(numerator * numerator, axis=0, keepdims=True) * (1.0 / DH)
        out_ref[heads, :] = (numerator * lax.rsqrt(mean + 1e-06)).astype(BF)


def mix(queries, inner, cumulative, far):
    return pl.pallas_call(
        mix_kernel,
        out_shape=jax.ShapeDtypeStruct((HEADS * DH, TOKENS), BF),
        in_specs=[VMEM] * 7,
        out_specs=VMEM,
        cost_estimate=cost(10**8, 4 * 10**6),
    )(queries, inner, cumulative, *[in_vmem(b) for b in far])


def piece_table(place_ref):
    c, xl = place_ref[0], place_ref[1]
    for hr in range(2):
        for z in range(8):
            for xr in range(2):
                h = c if hr == 0 else 1 - c
                x = xl if xr == 0 else 1 - xl
                yield hr * 16 + z * 2 + xr, 2 * (8 * x + z) + h, 4 * z + 2 * xr + h


def norm_kernel(place_ref, t0, t1, t2, t3, latent_ref, vector_ref, hidden_ref, normed_ref, work):
    sums = jnp.zeros((PADDED, SHARE), F32)
    for own, natural, term in piece_table(place_ref):
        attention = sum(t[term].astype(F32) for t in (t0, t1, t2, t3))
        hidden = latent_ref[natural].astype(F32) + vector_ref[natural][:, 3:4] * attention
        hidden_ref[own] = hidden
        sums = sums + hidden
    mean = jnp.sum(sums, axis=0, keepdims=True) * (1.0 / WIDTH)
    real = lax.broadcasted_iota(jnp.int32, (PADDED, SHARE), 0) < PIECE
    squares = jnp.zeros((PADDED, SHARE), F32)
    for own in range(PIECES):
        centered = hidden_ref[own] - mean
        squares = squares + centered * centered
    squares = jnp.where(real, squares, 0.0)
    scaling = lax.rsqrt(jnp.sum(squares, axis=0, keepdims=True) * (1.0 / WIDTH) + 1e-06)
    for own, natural, _ in piece_table(place_ref):
        vectors = vector_ref[natural]
        normed = (hidden_ref[own] - mean) * scaling * (1.0 + vectors[:, 1:2]) + vectors[:, 0:1]
        work[own * PADDED : (own + 1) * PADDED, :] = jnp.where(real, normed, 0.0)
    for i in range(ROWS // 256):
        normed_ref[:, 256 * i : 256 * (i + 1)] = work[256 * i : 256 * (i + 1), :].T.astype(BF)


def norm(place, terms, latents, vectors):
    return pl.pallas_call(
        norm_kernel,
        out_shape=(
            jax.ShapeDtypeStruct((PIECES, PADDED, SHARE), F32),
            jax.ShapeDtypeStruct((SHARE, ROWS), BF),
        ),
        in_specs=[SMEM] + [VMEM] * 6,
        out_specs=(VMEM, VMEM),
        scratch_shapes=[pltpu.VMEM((ROWS, SHARE), F32)],
        cost_estimate=cost(10**7, 8 * 10**6),
    )(place, *[in_vmem(t.reshape(PIECES, PADDED, SHARE)) for t in terms], latents, vectors)


def last_kernel(place_ref, step_ref, f0, f1, f2, f3, hidden_ref, latent_ref, vector_ref, v_ref, a_ref, v_work, a_work):
    step = step_ref[0]
    c, xl = place_ref[0], place_ref[1]
    for natural in range(PIECES):
        f, h = natural // 2, natural % 2
        hr = c if h == 0 else 1 - c
        xr = xl if f < 8 else 1 - xl
        own = hr * 16 + (f % 8) * 2 + xr
        feed = sum(f[own].astype(F32) for f in (f0, f1, f2, f3))
        velocity = (hidden_ref[own] + vector_ref[natural][:, 2:3] * feed).astype(BF).astype(F32)
        rows = slice(PIECE * natural, PIECE * (natural + 1))
        v_work[rows, :] = velocity[:PIECE]
        a_work[rows, :] = (latent_ref[natural].astype(F32) + step * velocity)[:PIECE]
    v_ref[...] = v_work[...].astype(BF)
    a_ref[...] = a_work[...].astype(BF)


def last(place, step_size, feeds, hidden, latents, vectors):
    shape = jax.ShapeDtypeStruct((WIDTH, SHARE), BF)
    return pl.pallas_call(
        last_kernel,
        out_shape=(shape, shape),
        in_specs=[SMEM] * 2 + [VMEM] * 7,
        out_specs=(VMEM, VMEM),
        scratch_shapes=[pltpu.VMEM((WIDTH, SHARE), F32)] * 2,
        cost_estimate=cost(10**7, 8 * 10**6),
    )(place, step_size, *[in_vmem(f.reshape(PIECES, PADDED, SHARE)) for f in feeds], hidden, latents, vectors)


HALF = ROWS // 2


def units_kernel(chunks, *refs):
    token_refs = refs[:chunks]
    own_ref, other_ref = refs[chunks : chunks + 2]
    out_refs = refs[chunks + 2 : 2 * chunks + 2]
    tokens, sums, units = refs[2 * chunks + 2 :]
    step = pl.program_id(0)

    def up(ref, first):
        weight = ref[...].reshape(HALF, -1)
        return jnp.dot(tokens[:, first : first + HALF], weight, preferred_element_type=F32)

    def down(ref):
        weight = ref[...].reshape(HALF, -1)
        feed = lax.dot_general(
            weight, units[...], (((1,), (1,)), ((), ())), preferred_element_type=F32
        ).astype(BF)
        for n in range(chunks):
            out_refs[n][...] = feed[:, SHARE * n : SHARE * (n + 1)]

    @pl.when(step == 0)
    def _():
        for n in range(chunks):
            tokens[SHARE * n : SHARE * (n + 1), :] = token_refs[n][...]
        sums[...] = up(own_ref, 0)

    @pl.when(step == 1)
    def _():
        units[...] = jax.nn.gelu(sums[...] + up(other_ref, HALF), approximate=True).astype(BF)

    @pl.when(step == 2)
    def _():
        down(own_ref)

    @pl.when(step == 3)
    def _():
        down(other_ref)


def unit_terms(tokens, own, other):
    chunks = len(tokens)
    hidden_units = own.shape[4]
    block = (8, 2, 1, PADDED, hidden_units)
    return pl.pallas_call(
        functools.partial(units_kernel, chunks),
        grid=(4,),
        out_shape=[jax.ShapeDtypeStruct((ROWS, SHARE), BF)] * chunks,
        in_specs=[pl.BlockSpec((SHARE, ROWS), lambda i: (0, 0))] * chunks
        + [
            pl.BlockSpec(block, lambda i: (0, 0, jnp.where(i >= 2, 1, 0), 0, 0)),
            pl.BlockSpec(block, lambda i: (0, 0, jnp.where(i >= 3, 1, 0), 0, 0)),
        ],
        out_specs=[pl.BlockSpec((HALF, SHARE), lambda i: (jnp.where(i >= 3, 1, 0), 0))] * chunks,
        scratch_shapes=[
            pltpu.VMEM((SHARE * chunks, ROWS), BF),
            pltpu.VMEM((SHARE * chunks, hidden_units), F32),
            pltpu.VMEM((SHARE * chunks, hidden_units), BF),
        ],
        cost_estimate=cost(4 * SHARE * chunks * ROWS * hidden_units, 4 * ROWS * hidden_units),
    )(*tokens, own, other)


def on_device(
    latents, queries, keys, values, log_decay, block_ids, t_index, w_mod, w_out, w_up, w_down
):
    y, c, xl = lax.axis_index("y"), lax.axis_index("c"), lax.axis_index("xl")
    place = jnp.stack([c, xl]).astype(jnp.int32)

    out_mine = padded_pieces(w_out.T).reshape(2 * PADDED, -1)
    out_pair = jnp.stack([out_mine, along_x(out_mine, 1)])
    out_weight = lax.all_gather(out_pair, "z", axis=0).reshape(ROWS, -1)
    both = jnp.stack([padded_pieces(w_up), padded_pieces(w_down.T)])
    mine = jnp.where(c == 0, both[:, 0], both[:, 1])

    queries, keys, values = queries.T, keys.T, values.T
    cumulative, packed = own_state(keys, values, log_decay)
    near = [along_frame(packed, d) for d in (1, 2, 3)]
    mine, _ = lax.optimization_barrier((mine, out_pair))
    mine_x = along_x(mine, 1)
    group = chain([packed] + near)
    far = [along_frame(group, d) for d in (1, 5, 9, 13)]
    mine, mine_x, _ = lax.optimization_barrier((mine, mine_x, group))
    pair = jnp.stack([mine, mine_x])
    half = lax.all_gather(pair, "z", axis=0)
    inner = inner_part(queries, keys, values, cumulative, block_ids[None, :])
    mixed = mix(queries, inner, cumulative, far)

    def head_terms(d):
        tokens = lax.dynamic_slice_in_dim(mixed, ((y + d) % 4) * SHARE, SHARE, axis=1)
        return jnp.dot(out_weight, tokens, preferred_element_type=F32).astype(BF)

    terms = [along_y(head_terms(d), d) for d in (2, 1, 3)] + [head_terms(0)]

    shifts, step_size = modulation_of(t_index, w_mod)
    vectors = padded_pieces(shifts.reshape(4, WIDTH).T)
    latent_pieces = padded_pieces(latents.T)
    hidden, normed = norm(place, terms, latent_pieces, vectors)

    theirs = {d: along_y(normed, -d) for d in (1, 3, 2)}
    half, _ = lax.optimization_barrier((half, theirs))
    other = other_core(half)
    near = unit_terms([theirs[1], theirs[3]], half, other)
    feeds = [along_y(near[0], 1), along_y(near[1], 3)]
    normed, _ = lax.optimization_barrier((normed, near[0]))
    rest = unit_terms([normed, theirs[2]], half, other)
    feeds += [rest[0], along_y(rest[1], 2)]
    step = step_size[None] if step_size.ndim == 0 else step_size
    velocity, advanced = last(place, step, feeds, hidden, latent_pieces, vectors)
    return (velocity.T, advanced.T)


def solution(mesh):
    fine = Mesh(mesh.devices.reshape(tuple(AXES.values())), tuple(AXES))
    pool, frame = ("xh", "c"), ("xl", "z")
    rows = P(pool + frame + ("y",), None)
    return jax.shard_map(
        on_device,
        mesh=fine,
        in_specs=(
            rows,
            P(pool + frame, "y"),
            P(pool + frame, "y"),
            P(pool + frame, "y"),
            P("y", pool + frame),
            P(pool + frame),
            P(pool),
            P(),
            P("y", frame),
            P(frame, "y"),
            P("y", frame),
        ),
        out_specs=(rows, rows),
        check_vma=False,
    )
```

```python
import functools
import math

import jax
import jax.numpy as jnp
import numpy as np
from jax import lax
from jax.experimental import pallas as pl
from jax.experimental.pallas import tpu as pltpu
from jax.sharding import Mesh, PartitionSpec as P


STEPS = 50
BF = jnp.bfloat16
F32 = jnp.float32
AXES = {"xh": 2, "c": 2, "xl": 2, "z": 8, "y": 4}
HEADS = 5
DH = 112
TOKENS = 512
SHARE = 128
WIDTH = 2240
PIECE = 70
PADDED = 72
PIECES = 32
ROWS = PIECES * PADDED
VMEM = pl.BlockSpec(memory_space=pltpu.VMEM)
SMEM = pl.BlockSpec(memory_space=pltpu.SMEM)


def permute(block, axes, route):
    sizes = [AXES[a] for a in axes]
    pairs = []
    for i in range(int(np.prod(sizes))):
        target = route(*[int(v) for v in np.unravel_index(i, sizes)])
        if target is not None:
            pairs.append((i, int(np.ravel_multi_index(target, sizes))))
    return lax.ppermute(block, tuple(axes) if len(axes) > 1 else axes[0], pairs)


def along_y(block, d):
    return permute(block, ("y",), lambda y: ((y + d) % 4,))


def along_x(block, d):
    def route(xh, xl):
        x = (2 * xh + xl + d) % 4
        return (x // 2, x % 2)

    return permute(block, ("xh", "xl"), route)


def other_core(block):
    return permute(block, ("c",), lambda c: (1 - c,))


def in_vmem(block):
    return pltpu.with_memory_space_constraint(block, pltpu.VMEM)


def cost(flops, size):
    return pl.CostEstimate(flops=flops, bytes_accessed=size, transcendentals=0)


def modulation_of(t_index, w_mod):
    fraction = 1.0 - t_index[0].astype(F32) / STEPS
    following = fraction - 1.0 / STEPS
    sigma_now = 3.0 * fraction / (1.0 + 2.0 * fraction)
    sigma_next = 3.0 * following / (1.0 + 2.0 * following)
    half_width = w_mod.shape[0] // 2
    frequency = jnp.exp(-math.log(10000.0) * jnp.arange(half_width).astype(F32) / half_width)
    angles = 1000.0 * sigma_now * frequency
    embedding = jnp.concatenate([jnp.cos(angles), jnp.sin(angles)])
    time_features = jax.nn.silu(embedding).astype(BF)
    shifts = jnp.dot(time_features[None, :], w_mod, preferred_element_type=F32)[0]
    return (lax.optimization_barrier(shifts), sigma_next - sigma_now)


def padded_pieces(rows):
    pieces = rows.reshape(-1, PIECE, rows.shape[1])
    return jnp.pad(pieces, ((0, 0), (0, PADDED - PIECE), (0, 0)))


STATE_ROWS = 640


def total_lanes(total):
    hi = total.astype(BF).astype(F32)
    mid = (total - hi).astype(BF).astype(F32)
    low = total - hi - mid
    lane = lax.broadcasted_iota(jnp.int32, (DH, 16), 1)
    zero = jnp.zeros((DH, 16), F32)
    return jnp.where(lane == 0, hi, jnp.where(lane == 1, mid, jnp.where(lane == 2, low, zero))).astype(BF)


def state_kernel(k_ref, v_ref, decay_ref, cumulative_ref, packed_ref):
    decay = decay_ref[...]
    hi = decay.astype(BF)
    rest = decay - hi.astype(F32)
    mid = rest.astype(BF)
    low = (rest - mid.astype(F32)).astype(BF)
    row = lax.broadcasted_iota(jnp.int32, (TOKENS, TOKENS), 0)
    column = lax.broadcasted_iota(jnp.int32, (TOKENS, TOKENS), 1)
    triangle = jnp.where(row <= column, 1.0, 0.0).astype(BF)
    cumulative = sum(
        jnp.dot(part, triangle, preferred_element_type=F32) for part in (low, mid, hi)
    )
    cumulative_ref[...] = cumulative
    for h in range(HEADS):
        mine = cumulative[h : h + 1, :]
        total = mine[:, TOKENS - 1 :]
        heads = pl.ds(DH * h, DH)
        scaled = (k_ref[heads, :].astype(F32) * jnp.exp(total - mine)).astype(BF)
        state = lax.dot_general(
            v_ref[heads, :], scaled, (((1,), (1,)), ((), ())), preferred_element_type=F32
        )
        packed_ref[heads, 0:DH] = state.astype(BF)
        packed_ref[heads, DH:SHARE] = total_lanes(total)
    packed_ref[HEADS * DH :, :] = jnp.zeros((STATE_ROWS - HEADS * DH, SHARE), BF)


def own_state(keys, values, log_decay):
    return pl.pallas_call(
        state_kernel,
        out_shape=(
            jax.ShapeDtypeStruct((HEADS, TOKENS), F32),
            jax.ShapeDtypeStruct((STATE_ROWS, SHARE), BF),
        ),
        in_specs=[VMEM] * 3,
        out_specs=(VMEM, VMEM),
        cost_estimate=cost(10**9, 3 * 10**6),
    )(keys, values, log_decay)


def scan_kernel(blocks_ref, before_ref):
    state = jnp.zeros(before_ref.shape[1:], F32)
    for f in range(blocks_ref.shape[0]):
        before_ref[f] = state.astype(BF)
        packed = blocks_ref[f].astype(F32)
        total = jnp.sum(packed[:, DH : DH + 3], axis=1, keepdims=True)
        state = packed + jnp.exp(total) * state


def scan_blocks(blocks):
    return pl.pallas_call(
        scan_kernel,
        out_shape=jax.ShapeDtypeStruct(blocks.shape, BF),
        in_specs=[VMEM],
        out_specs=VMEM,
        cost_estimate=cost(10**6, 10**6),
    )(in_vmem(blocks))


def inner_kernel(q_ref, k_ref, v_ref, cumulative_ref, labels_ref, out_ref):
    cumulative = cumulative_ref[...]
    labels = labels_ref[...].astype(F32)
    stacked = jnp.concatenate([cumulative, labels, jnp.zeros((2, TOKENS), F32)], axis=0)
    columns = stacked.T
    visible = columns[:, HEADS : HEADS + 1] <= labels
    for h in range(HEADS):
        heads = pl.ds(DH * h, DH)
        scores = lax.dot_general(
            k_ref[heads, :], q_ref[heads, :], (((0,), (0,)), ((), ())), preferred_element_type=F32
        )
        decay = jnp.exp(jnp.minimum(cumulative[h : h + 1, :] - columns[:, h : h + 1], 0.0))
        weights = jnp.where(visible, decay * (DH**-0.5), 0.0)
        probs = (scores * weights).astype(BF)
        out_ref[heads, :] = jnp.dot(v_ref[heads, :], probs, preferred_element_type=F32)


def inner_part(queries, keys, values, cumulative, labels):
    return pl.pallas_call(
        inner_kernel,
        out_shape=jax.ShapeDtypeStruct((HEADS * DH, TOKENS), F32),
        in_specs=[VMEM] * 5,
        out_specs=VMEM,
        cost_estimate=cost(5 * 10**9, 4 * 10**6),
    )(queries, keys, values, cumulative, labels)


def mix_kernel(q_ref, inner_ref, cumulative_ref, before_ref, out_ref):
    for h in range(HEADS):
        heads = pl.ds(DH * h, DH)
        carried = jnp.dot(
            before_ref[heads, :][:, 0:DH], q_ref[heads, :], preferred_element_type=F32
        )
        numerator = inner_ref[heads, :] + carried * (
            jnp.exp(cumulative_ref[h : h + 1, :]) * (DH**-0.5)
        )
        mean = jnp.sum(numerator * numerator, axis=0, keepdims=True) * (1.0 / DH)
        out_ref[heads, :] = (numerator * lax.rsqrt(mean + 1e-06)).astype(BF)


def mix(queries, inner, cumulative, before):
    return pl.pallas_call(
        mix_kernel,
        out_shape=jax.ShapeDtypeStruct((HEADS * DH, TOKENS), BF),
        in_specs=[VMEM] * 4,
        out_specs=VMEM,
        cost_estimate=cost(10**8, 4 * 10**6),
    )(queries, inner, cumulative, in_vmem(before))


def piece_table(place_ref):
    c, xl = place_ref[0], place_ref[1]
    for hr in range(2):
        for z in range(8):
            for xr in range(2):
                h = c if hr == 0 else 1 - c
                x = xl if xr == 0 else 1 - xl
                yield hr * 16 + z * 2 + xr, 2 * (8 * x + z) + h, 4 * z + 2 * xr + h


def norm_kernel(place_ref, t0, t1, t2, t3, latent_ref, vector_ref, hidden_ref, normed_ref, work):
    sums = jnp.zeros((PADDED, SHARE), F32)
    for own, natural, term in piece_table(place_ref):
        attention = sum(t[term].astype(F32) for t in (t0, t1, t2, t3))
        hidden = latent_ref[natural].astype(F32) + vector_ref[natural][:, 3:4] * attention
        hidden_ref[own] = hidden
        sums = sums + hidden
    mean = jnp.sum(sums, axis=0, keepdims=True) * (1.0 / WIDTH)
    real = lax.broadcasted_iota(jnp.int32, (PADDED, SHARE), 0) < PIECE
    squares = jnp.zeros((PADDED, SHARE), F32)
    for own in range(PIECES):
        centered = hidden_ref[own] - mean
        squares = squares + centered * centered
    squares = jnp.where(real, squares, 0.0)
    scaling = lax.rsqrt(jnp.sum(squares, axis=0, keepdims=True) * (1.0 / WIDTH) + 1e-06)
    for own, natural, _ in piece_table(place_ref):
        vectors = vector_ref[natural]
        normed = (hidden_ref[own] - mean) * scaling * (1.0 + vectors[:, 1:2]) + vectors[:, 0:1]
        work[own * PADDED : (own + 1) * PADDED, :] = jnp.where(real, normed, 0.0)
    for i in range(ROWS // 256):
        normed_ref[:, 256 * i : 256 * (i + 1)] = work[256 * i : 256 * (i + 1), :].T.astype(BF)


def norm(place, terms, latents, vectors):
    return pl.pallas_call(
        norm_kernel,
        out_shape=(
            jax.ShapeDtypeStruct((PIECES, PADDED, SHARE), F32),
            jax.ShapeDtypeStruct((SHARE, ROWS), BF),
        ),
        in_specs=[SMEM] + [VMEM] * 6,
        out_specs=(VMEM, VMEM),
        scratch_shapes=[pltpu.VMEM((ROWS, SHARE), F32)],
        cost_estimate=cost(10**7, 8 * 10**6),
    )(place, *[in_vmem(t.reshape(PIECES, PADDED, SHARE)) for t in terms], latents, vectors)


def last_kernel(place_ref, step_ref, f0, f1, f2, f3, hidden_ref, latent_ref, vector_ref, v_ref, a_ref, v_work, a_work):
    step = step_ref[0]
    c, xl = place_ref[0], place_ref[1]
    for natural in range(PIECES):
        f, h = natural // 2, natural % 2
        hr = c if h == 0 else 1 - c
        xr = xl if f < 8 else 1 - xl
        own = hr * 16 + (f % 8) * 2 + xr
        feed = sum(f[own].astype(F32) for f in (f0, f1, f2, f3))
        velocity = (hidden_ref[own] + vector_ref[natural][:, 2:3] * feed).astype(BF).astype(F32)
        rows = slice(PIECE * natural, PIECE * (natural + 1))
        v_work[rows, :] = velocity[:PIECE]
        a_work[rows, :] = (latent_ref[natural].astype(F32) + step * velocity)[:PIECE]
    v_ref[...] = v_work[...].astype(BF)
    a_ref[...] = a_work[...].astype(BF)


def last(place, step_size, feeds, hidden, latents, vectors):
    shape = jax.ShapeDtypeStruct((WIDTH, SHARE), BF)
    return pl.pallas_call(
        last_kernel,
        out_shape=(shape, shape),
        in_specs=[SMEM] * 2 + [VMEM] * 7,
        out_specs=(VMEM, VMEM),
        scratch_shapes=[pltpu.VMEM((WIDTH, SHARE), F32)] * 2,
        cost_estimate=cost(10**7, 8 * 10**6),
    )(place, step_size, *[in_vmem(f.reshape(PIECES, PADDED, SHARE)) for f in feeds], hidden, latents, vectors)


HALF = ROWS // 2


def units_kernel(chunks, *refs):
    token_refs = refs[:chunks]
    own_ref, other_ref = refs[chunks : chunks + 2]
    out_refs = refs[chunks + 2 : 2 * chunks + 2]
    tokens, sums, units = refs[2 * chunks + 2 :]
    step = pl.program_id(0)

    def up(ref, first):
        weight = ref[...].reshape(HALF, -1)
        return jnp.dot(tokens[:, first : first + HALF], weight, preferred_element_type=F32)

    def down(ref):
        weight = ref[...].reshape(HALF, -1)
        feed = lax.dot_general(
            weight, units[...], (((1,), (1,)), ((), ())), preferred_element_type=F32
        ).astype(BF)
        for n in range(chunks):
            out_refs[n][...] = feed[:, SHARE * n : SHARE * (n + 1)]

    @pl.when(step == 0)
    def _():
        for n in range(chunks):
            tokens[SHARE * n : SHARE * (n + 1), :] = token_refs[n][...]
        sums[...] = up(own_ref, 0)

    @pl.when(step == 1)
    def _():
        units[...] = jax.nn.gelu(sums[...] + up(other_ref, HALF), approximate=True).astype(BF)

    @pl.when(step == 2)
    def _():
        down(own_ref)

    @pl.when(step == 3)
    def _():
        down(other_ref)


def unit_terms(tokens, own, other):
    chunks = len(tokens)
    hidden_units = own.shape[4]
    block = (8, 2, 1, PADDED, hidden_units)
    return pl.pallas_call(
        functools.partial(units_kernel, chunks),
        grid=(4,),
        out_shape=[jax.ShapeDtypeStruct((ROWS, SHARE), BF)] * chunks,
        in_specs=[pl.BlockSpec((SHARE, ROWS), lambda i: (0, 0))] * chunks
        + [
            pl.BlockSpec(block, lambda i: (0, 0, jnp.where(i >= 2, 1, 0), 0, 0)),
            pl.BlockSpec(block, lambda i: (0, 0, jnp.where(i >= 3, 1, 0), 0, 0)),
        ],
        out_specs=[pl.BlockSpec((HALF, SHARE), lambda i: (jnp.where(i >= 3, 1, 0), 0))] * chunks,
        scratch_shapes=[
            pltpu.VMEM((SHARE * chunks, ROWS), BF),
            pltpu.VMEM((SHARE * chunks, hidden_units), F32),
            pltpu.VMEM((SHARE * chunks, hidden_units), BF),
        ],
        cost_estimate=cost(4 * SHARE * chunks * ROWS * hidden_units, 4 * ROWS * hidden_units),
    )(*tokens, own, other)


def block(
    latents, queries, keys, values, log_decay, block_ids, t_index, w_mod, w_out, w_up, w_down
):
    y, c, xl = lax.axis_index("y"), lax.axis_index("c"), lax.axis_index("xl")
    place = jnp.stack([c, xl]).astype(jnp.int32)

    out_mine = padded_pieces(w_out.T).reshape(2 * PADDED, -1)
    out_pair = jnp.stack([out_mine, along_x(out_mine, 1)])
    out_weight = lax.all_gather(out_pair, "z", axis=0).reshape(ROWS, -1)
    both = jnp.stack([padded_pieces(w_up), padded_pieces(w_down.T)])
    mine = jnp.where(c == 0, both[:, 0], both[:, 1])

    queries, keys, values = queries.T, keys.T, values.T
    cumulative, packed = own_state(keys, values, log_decay)
    slices = lax.all_to_all(packed.reshape(16, -1, SHARE), ("xl", "z"), 0, 0)
    mine, _ = lax.optimization_barrier((mine, slices))
    mine_x = along_x(mine, 1)
    ahead = scan_blocks(slices)
    before = lax.all_to_all(ahead, ("xl", "z"), 0, 0).reshape(STATE_ROWS, SHARE)
    mine, mine_x, _ = lax.optimization_barrier((mine, mine_x, before))
    pair = jnp.stack([mine, mine_x])
    half = lax.all_gather(pair, "z", axis=0)
    inner = inner_part(queries, keys, values, cumulative, block_ids[None, :])
    mixed = mix(queries, inner, cumulative, before)

    def head_terms(d):
        tokens = lax.dynamic_slice_in_dim(mixed, ((y + d) % 4) * SHARE, SHARE, axis=1)
        return jnp.dot(out_weight, tokens, preferred_element_type=F32).astype(BF)

    terms = [along_y(head_terms(d), d) for d in (2, 1, 3)] + [head_terms(0)]

    shifts, step_size = modulation_of(t_index, w_mod)
    vectors = padded_pieces(shifts.reshape(4, WIDTH).T)
    latent_pieces = padded_pieces(latents.T)
    hidden, normed = norm(place, terms, latent_pieces, vectors)

    theirs = {d: along_y(normed, -d) for d in (1, 3, 2)}
    half, _ = lax.optimization_barrier((half, theirs))
    other = other_core(half)
    near = unit_terms([theirs[1], theirs[3]], half, other)
    feeds = []
    for d, part in zip((1, 3), near):
        feeds.append(along_y(part, d))
    normed, _ = lax.optimization_barrier((normed, near[0]))
    rest = unit_terms([normed, theirs[2]], half, other)
    feeds += [rest[0], along_y(rest[1], 2)]
    step = step_size[None] if step_size.ndim == 0 else step_size
    velocity, advanced = last(place, step, feeds, hidden, latent_pieces, vectors)
    return (velocity.T, advanced.T)


def solution(mesh):
    fine = Mesh(mesh.devices.reshape(tuple(AXES.values())), tuple(AXES))
    pool, frame = ("xh", "c"), ("xl", "z")
    rows = P(pool + frame + ("y",), None)
    return jax.shard_map(
        block,
        mesh=fine,
        in_specs=(
            rows,
            P(pool + frame, "y"),
            P(pool + frame, "y"),
            P(pool + frame, "y"),
            P("y", pool + frame),
            P(pool + frame),
            P(pool),
            P(),
            P("y", frame),
            P(frame, "y"),
            P("y", frame),
        ),
        out_specs=(rows, rows),
        check_vma=False,
    )
```

```python
import functools
import math

import jax
import jax.numpy as jnp
import numpy as np
from jax import lax
from jax.experimental import pallas as pl
from jax.experimental.pallas import tpu as pltpu
from jax.sharding import Mesh, PartitionSpec as P


STEPS = 50
BF = jnp.bfloat16
F32 = jnp.float32
AXES = {"xh": 2, "c": 2, "xl": 2, "z": 8, "y": 4}
HEADS = 5
DH = 112
TOKENS = 512
SHARE = 128
WIDTH = 2240
PIECE = 70
PADDED = 72
PIECES = 32
ROWS = PIECES * PADDED
VMEM = pl.BlockSpec(memory_space=pltpu.VMEM)
SMEM = pl.BlockSpec(memory_space=pltpu.SMEM)


def permute(block, axes, route):
    sizes = [AXES[a] for a in axes]
    pairs = []
    for i in range(int(np.prod(sizes))):
        target = route(*[int(v) for v in np.unravel_index(i, sizes)])
        if target is not None:
            pairs.append((i, int(np.ravel_multi_index(target, sizes))))
    return lax.ppermute(block, tuple(axes) if len(axes) > 1 else axes[0], pairs)


def along_y(block, d):
    return permute(block, ("y",), lambda y: ((y + d) % 4,))


def along_x(block, d):
    def route(xh, xl):
        x = (2 * xh + xl + d) % 4
        return (x // 2, x % 2)

    return permute(block, ("xh", "xl"), route)


def other_core(block):
    return permute(block, ("c",), lambda c: (1 - c,))


def in_vmem(block):
    return pltpu.with_memory_space_constraint(block, pltpu.VMEM)


def cost(flops, size):
    return pl.CostEstimate(flops=flops, bytes_accessed=size, transcendentals=0)


def modulation_of(t_index, w_mod):
    fraction = 1.0 - t_index[0].astype(F32) / STEPS
    following = fraction - 1.0 / STEPS
    sigma_now = 3.0 * fraction / (1.0 + 2.0 * fraction)
    sigma_next = 3.0 * following / (1.0 + 2.0 * following)
    half_width = w_mod.shape[0] // 2
    frequency = jnp.exp(-math.log(10000.0) * jnp.arange(half_width).astype(F32) / half_width)
    angles = 1000.0 * sigma_now * frequency
    embedding = jnp.concatenate([jnp.cos(angles), jnp.sin(angles)])
    time_features = jax.nn.silu(embedding).astype(BF)
    shifts = jnp.dot(time_features[None, :], w_mod, preferred_element_type=F32)[0]
    return (lax.optimization_barrier(shifts), sigma_next - sigma_now)


def padded_pieces(rows):
    pieces = rows.reshape(-1, PIECE, rows.shape[1])
    return jnp.pad(pieces, ((0, 0), (0, PADDED - PIECE), (0, 0)))


STATE_ROWS = 640


def total_lanes(total):
    hi = total.astype(BF).astype(F32)
    mid = (total - hi).astype(BF).astype(F32)
    low = total - hi - mid
    lane = lax.broadcasted_iota(jnp.int32, (DH, 16), 1)
    zero = jnp.zeros((DH, 16), F32)
    return jnp.where(lane == 0, hi, jnp.where(lane == 1, mid, jnp.where(lane == 2, low, zero))).astype(BF)


def state_kernel(k_ref, v_ref, decay_ref, cumulative_ref, packed_ref):
    decay = decay_ref[...]
    hi = decay.astype(BF)
    rest = decay - hi.astype(F32)
    mid = rest.astype(BF)
    low = (rest - mid.astype(F32)).astype(BF)
    row = lax.broadcasted_iota(jnp.int32, (TOKENS, TOKENS), 0)
    column = lax.broadcasted_iota(jnp.int32, (TOKENS, TOKENS), 1)
    triangle = jnp.where(row <= column, 1.0, 0.0).astype(BF)
    cumulative = sum(
        jnp.dot(part, triangle, preferred_element_type=F32) for part in (low, mid, hi)
    )
    cumulative_ref[...] = cumulative
    for h in range(HEADS):
        mine = cumulative[h : h + 1, :]
        total = mine[:, TOKENS - 1 :]
        heads = pl.ds(DH * h, DH)
        scaled = (k_ref[heads, :].astype(F32) * jnp.exp(total - mine)).astype(BF)
        state = lax.dot_general(
            v_ref[heads, :], scaled, (((1,), (1,)), ((), ())), preferred_element_type=F32
        )
        packed_ref[heads, 0:DH] = state.astype(BF)
        packed_ref[heads, DH:SHARE] = total_lanes(total)
    packed_ref[HEADS * DH :, :] = jnp.zeros((STATE_ROWS - HEADS * DH, SHARE), BF)


def own_state(keys, values, log_decay):
    return pl.pallas_call(
        state_kernel,
        out_shape=(
            jax.ShapeDtypeStruct((HEADS, TOKENS), F32),
            jax.ShapeDtypeStruct((STATE_ROWS, SHARE), BF),
        ),
        in_specs=[VMEM] * 3,
        out_specs=(VMEM, VMEM),
        cost_estimate=cost(10**9, 3 * 10**6),
    )(keys, values, log_decay)


def scan_kernel(blocks_ref, before_ref):
    state = jnp.zeros(before_ref.shape[1:], F32)
    for f in range(blocks_ref.shape[0]):
        before_ref[f] = state.astype(BF)
        packed = blocks_ref[f].astype(F32)
        total = jnp.sum(packed[:, DH : DH + 3], axis=1, keepdims=True)
        state = packed + jnp.exp(total) * state


def scan_blocks(blocks):
    return pl.pallas_call(
        scan_kernel,
        out_shape=jax.ShapeDtypeStruct(blocks.shape, BF),
        in_specs=[VMEM],
        out_specs=VMEM,
        cost_estimate=cost(10**6, 10**6),
    )(in_vmem(blocks))


def inner_kernel(q_ref, k_ref, v_ref, cumulative_ref, labels_ref, out_ref):
    cumulative = cumulative_ref[...]
    labels = labels_ref[...].astype(F32)
    stacked = jnp.concatenate([cumulative, labels, jnp.zeros((2, TOKENS), F32)], axis=0)
    columns = stacked.T
    visible = columns[:, HEADS : HEADS + 1] <= labels
    for h in range(HEADS):
        heads = pl.ds(DH * h, DH)
        scores = lax.dot_general(
            k_ref[heads, :], q_ref[heads, :], (((0,), (0,)), ((), ())), preferred_element_type=F32
        )
        decay = jnp.exp(jnp.minimum(cumulative[h : h + 1, :] - columns[:, h : h + 1], 0.0))
        weights = jnp.where(visible, decay * (DH**-0.5), 0.0)
        probs = (scores * weights).astype(BF)
        out_ref[heads, :] = jnp.dot(v_ref[heads, :], probs, preferred_element_type=F32)


def inner_part(queries, keys, values, cumulative, labels):
    return pl.pallas_call(
        inner_kernel,
        out_shape=jax.ShapeDtypeStruct((HEADS * DH, TOKENS), F32),
        in_specs=[VMEM] * 5,
        out_specs=VMEM,
        cost_estimate=cost(5 * 10**9, 4 * 10**6),
    )(queries, keys, values, cumulative, labels)


def mix_kernel(q_ref, inner_ref, cumulative_ref, before_ref, out_ref):
    for h in range(HEADS):
        heads = pl.ds(DH * h, DH)
        carried = jnp.dot(
            before_ref[heads, :][:, 0:DH], q_ref[heads, :], preferred_element_type=F32
        )
        numerator = inner_ref[heads, :] + carried * (
            jnp.exp(cumulative_ref[h : h + 1, :]) * (DH**-0.5)
        )
        mean = jnp.sum(numerator * numerator, axis=0, keepdims=True) * (1.0 / DH)
        out_ref[heads, :] = (numerator * lax.rsqrt(mean + 1e-06)).astype(BF)


def mix(queries, inner, cumulative, before):
    return pl.pallas_call(
        mix_kernel,
        out_shape=jax.ShapeDtypeStruct((HEADS * DH, TOKENS), BF),
        in_specs=[VMEM] * 4,
        out_specs=VMEM,
        cost_estimate=cost(10**8, 4 * 10**6),
    )(queries, inner, cumulative, in_vmem(before))


FARTHEST_FIRST = (2, 1, 3, 0)


def head_kernel(place_ref, mixed_ref, own_ref, first_ref, second_ref, *out_refs):
    for d, out_ref in zip(FARTHEST_FIRST, out_refs):
        start = pl.multiple_of(((place_ref[2] + d) % 4) * SHARE, SHARE)
        tokens = mixed_ref[:, pl.ds(start, SHARE)]
        row = 0
        for weight_ref in (own_ref, first_ref, second_ref):
            weight = weight_ref[...].reshape(-1, weight_ref.shape[2])
            rows = weight.shape[0]
            out_ref[row : row + rows, :] = jnp.dot(
                weight, tokens, preferred_element_type=F32
            ).astype(BF)
            row += rows


def head_terms(place, mixed, weights):
    return pl.pallas_call(
        head_kernel,
        out_shape=[jax.ShapeDtypeStruct((ROWS, SHARE), BF)] * 4,
        in_specs=[SMEM] + [VMEM] * 4,
        out_specs=[VMEM] * 4,
        cost_estimate=cost(2 * 10**9, 5 * 10**6),
    )(place, mixed, weights[0], *[in_vmem(w) for w in weights[1:]])


def piece_table(place_ref):
    c, xl = place_ref[0], place_ref[1]
    for hr in range(2):
        for z in range(8):
            for xr in range(2):
                h = c if hr == 0 else 1 - c
                x = xl if xr == 0 else 1 - xl
                yield hr * 16 + z * 2 + xr, 2 * (8 * x + z) + h, 16 * xr + 2 * z + h


def norm_kernel(place_ref, t0, t1, t2, t3, latent_ref, vector_ref, hidden_ref, normed_ref, work):
    sums = jnp.zeros((PADDED, SHARE), F32)
    for own, natural, term in piece_table(place_ref):
        attention = sum(t[term].astype(F32) for t in (t0, t1, t2, t3))
        hidden = latent_ref[natural].astype(F32) + vector_ref[natural][:, 3:4] * attention
        hidden_ref[own] = hidden
        sums = sums + hidden
    mean = jnp.sum(sums, axis=0, keepdims=True) * (1.0 / WIDTH)
    real = lax.broadcasted_iota(jnp.int32, (PADDED, SHARE), 0) < PIECE
    squares = jnp.zeros((PADDED, SHARE), F32)
    for own in range(PIECES):
        centered = hidden_ref[own] - mean
        squares = squares + centered * centered
    squares = jnp.where(real, squares, 0.0)
    scaling = lax.rsqrt(jnp.sum(squares, axis=0, keepdims=True) * (1.0 / WIDTH) + 1e-06)
    for own, natural, _ in piece_table(place_ref):
        vectors = vector_ref[natural]
        normed = (hidden_ref[own] - mean) * scaling * (1.0 + vectors[:, 1:2]) + vectors[:, 0:1]
        work[own * PADDED : (own + 1) * PADDED, :] = jnp.where(real, normed, 0.0)
    for i in range(ROWS // 256):
        normed_ref[:, 256 * i : 256 * (i + 1)] = work[256 * i : 256 * (i + 1), :].T.astype(BF)


def arrived(parts):
    pieces = [p.reshape(PIECES, PADDED, SHARE) for p in parts]
    return [in_vmem(p) for p in pieces[:-1]] + pieces[-1:]


def norm(place, terms, latents, vectors):
    return pl.pallas_call(
        norm_kernel,
        out_shape=(
            jax.ShapeDtypeStruct((PIECES, PADDED, SHARE), F32),
            jax.ShapeDtypeStruct((SHARE, ROWS), BF),
        ),
        in_specs=[SMEM] + [VMEM] * 6,
        out_specs=(VMEM, VMEM),
        scratch_shapes=[pltpu.VMEM((ROWS, SHARE), F32)],
        cost_estimate=cost(10**7, 8 * 10**6),
    )(place, *arrived(terms), latents, vectors)


def last_kernel(place_ref, step_ref, f0, f1, f2, f3, hidden_ref, latent_ref, vector_ref, v_ref, a_ref, v_work, a_work):
    step = step_ref[0]
    c, xl = place_ref[0], place_ref[1]
    for natural in range(PIECES):
        f, h = natural // 2, natural % 2
        hr = c if h == 0 else 1 - c
        xr = xl if f < 8 else 1 - xl
        own = hr * 16 + (f % 8) * 2 + xr
        feed = sum(f[own].astype(F32) for f in (f0, f1, f2, f3))
        velocity = (hidden_ref[own] + vector_ref[natural][:, 2:3] * feed).astype(BF).astype(F32)
        rows = slice(PIECE * natural, PIECE * (natural + 1))
        v_work[rows, :] = velocity[:PIECE]
        a_work[rows, :] = (latent_ref[natural].astype(F32) + step * velocity)[:PIECE]
    v_ref[...] = v_work[...].astype(BF)
    a_ref[...] = a_work[...].astype(BF)


def last(place, step_size, feeds, hidden, latents, vectors):
    shape = jax.ShapeDtypeStruct((WIDTH, SHARE), BF)
    return pl.pallas_call(
        last_kernel,
        out_shape=(shape, shape),
        in_specs=[SMEM] * 2 + [VMEM] * 7,
        out_specs=(VMEM, VMEM),
        scratch_shapes=[pltpu.VMEM((WIDTH, SHARE), F32)] * 2,
        cost_estimate=cost(10**7, 8 * 10**6),
    )(place, step_size, *arrived(feeds), hidden, latents, vectors)


HALF = ROWS // 2


def units_kernel(chunks, *refs):
    token_refs = refs[:chunks]
    own_ref, other_ref = refs[chunks : chunks + 2]
    out_refs = refs[chunks + 2 : 2 * chunks + 2]
    tokens, sums, units = refs[2 * chunks + 2 :]
    step = pl.program_id(0)

    def up(ref, first):
        weight = ref[...].reshape(HALF, -1)
        return jnp.dot(tokens[:, first : first + HALF], weight, preferred_element_type=F32)

    def down(ref):
        weight = ref[...].reshape(HALF, -1)
        feed = lax.dot_general(
            weight, units[...], (((1,), (1,)), ((), ())), preferred_element_type=F32
        ).astype(BF)
        for n in range(chunks):
            out_refs[n][...] = feed[:, SHARE * n : SHARE * (n + 1)]

    @pl.when(step == 0)
    def _():
        for n in range(chunks):
            tokens[SHARE * n : SHARE * (n + 1), :] = token_refs[n][...]
        sums[...] = up(own_ref, 0)

    @pl.when(step == 1)
    def _():
        units[...] = jax.nn.gelu(sums[...] + up(other_ref, HALF), approximate=True).astype(BF)

    @pl.when(step == 2)
    def _():
        down(own_ref)

    @pl.when(step == 3)
    def _():
        down(other_ref)


def unit_terms(tokens, own, other):
    chunks = len(tokens)
    hidden_units = own.shape[4]
    block = (8, 2, 1, PADDED, hidden_units)
    return pl.pallas_call(
        functools.partial(units_kernel, chunks),
        grid=(4,),
        out_shape=[jax.ShapeDtypeStruct((ROWS, SHARE), BF)] * chunks,
        in_specs=[pl.BlockSpec((SHARE, ROWS), lambda i: (0, 0))] * chunks
        + [
            pl.BlockSpec(block, lambda i: (0, 0, jnp.where(i >= 2, 1, 0), 0, 0)),
            pl.BlockSpec(block, lambda i: (0, 0, jnp.where(i >= 3, 1, 0), 0, 0)),
        ],
        out_specs=[pl.BlockSpec((HALF, SHARE), lambda i: (jnp.where(i >= 3, 1, 0), 0))] * chunks,
        scratch_shapes=[
            pltpu.VMEM((SHARE * chunks, ROWS), BF),
            pltpu.VMEM((SHARE * chunks, hidden_units), F32),
            pltpu.VMEM((SHARE * chunks, hidden_units), BF),
        ],
        cost_estimate=cost(4 * SHARE * chunks * ROWS * hidden_units, 4 * ROWS * hidden_units),
    )(*tokens, own, other)


def block(
    latents, queries, keys, values, log_decay, block_ids, t_index, w_mod, w_out, w_up, w_down
):
    y, c, xl = lax.axis_index("y"), lax.axis_index("c"), lax.axis_index("xl")
    place = jnp.stack([c, xl, y]).astype(jnp.int32)

    out_mine = padded_pieces(w_out.T).reshape(2 * PADDED, -1)
    out_own = lax.all_gather(out_mine, "z", axis=0)
    out_first, out_second = along_x(out_own[:4], 1), along_x(out_own[4:], -1)
    both = jnp.stack([padded_pieces(w_up), padded_pieces(w_down.T)])
    mine = jnp.where(c == 0, both[:, 0], both[:, 1])

    queries, keys, values = queries.T, keys.T, values.T
    cumulative, packed = own_state(keys, values, log_decay)
    slices = lax.all_to_all(packed.reshape(16, -1, SHARE), ("xl", "z"), 0, 0)
    mine, _ = lax.optimization_barrier((mine, slices))
    mine_x = along_x(mine, 1)
    ahead = scan_blocks(slices)
    before = lax.all_to_all(ahead, ("xl", "z"), 0, 0).reshape(STATE_ROWS, SHARE)
    mine, mine_x, _ = lax.optimization_barrier((mine, mine_x, before))
    pair = jnp.stack([mine, mine_x])
    half = lax.all_gather(pair, "z", axis=0)
    inner = inner_part(queries, keys, values, cumulative, block_ids[None, :])
    mixed = mix(queries, inner, cumulative, before)

    parts = head_terms(place, mixed, [out_own, out_first, out_second])
    terms = [along_y(parts[i], d) for i, d in enumerate(FARTHEST_FIRST[:3])] + [parts[3]]

    shifts, step_size = modulation_of(t_index, w_mod)
    vectors = padded_pieces(shifts.reshape(4, WIDTH).T)
    latent_pieces = padded_pieces(latents.T)
    hidden, normed = norm(place, terms, latent_pieces, vectors)

    theirs = {d: along_y(normed, -d) for d in (1, 3)}
    theirs[2] = along_y(normed, -2)
    half, _ = lax.optimization_barrier((half, (theirs[1], theirs[3])))
    other = other_core(half)
    near = unit_terms([theirs[1], theirs[3]], half, other)
    feeds = []
    for d, part in zip((1, 3), near):
        feeds.append(along_y(part, d))
    normed, _ = lax.optimization_barrier((normed, near[0]))
    rest = unit_terms([normed, theirs[2]], half, other)
    feeds += [along_y(rest[1], 2), rest[0]]
    step = step_size[None] if step_size.ndim == 0 else step_size
    velocity, advanced = last(place, step, feeds, hidden, latent_pieces, vectors)
    return (velocity.T, advanced.T)


def solution(mesh):
    fine = Mesh(mesh.devices.reshape(tuple(AXES.values())), tuple(AXES))
    pool, frame = ("xh", "c"), ("xl", "z")
    rows = P(pool + frame + ("y",), None)
    return jax.shard_map(
        block,
        mesh=fine,
        in_specs=(
            rows,
            P(pool + frame, "y"),
            P(pool + frame, "y"),
            P(pool + frame, "y"),
            P("y", pool + frame),
            P(pool + frame),
            P(pool),
            P(),
            P("y", frame),
            P(frame, "y"),
            P("y", frame),
        ),
        out_specs=(rows, rows),
        check_vma=False,
    )
```

```python
import functools
import math

import jax
import jax.numpy as jnp
import numpy as np
from jax import lax
from jax.experimental import pallas as pl
from jax.experimental.pallas import tpu as pltpu
from jax.sharding import Mesh, PartitionSpec as P


STEPS = 50
BF = jnp.bfloat16
F32 = jnp.float32
AXES = {"xh": 2, "c": 2, "xl": 2, "z": 8, "y": 4}
HEADS = 5
DH = 112
TOKENS = 512
SHARE = 128
WIDTH = 2240
PIECE = 70
PADDED = 72
PIECES = 32
ROWS = PIECES * PADDED
VMEM = pl.BlockSpec(memory_space=pltpu.VMEM)
SMEM = pl.BlockSpec(memory_space=pltpu.SMEM)


def permute(block, axes, route):
    sizes = [AXES[a] for a in axes]
    pairs = []
    for i in range(int(np.prod(sizes))):
        target = route(*[int(v) for v in np.unravel_index(i, sizes)])
        if target is not None:
            pairs.append((i, int(np.ravel_multi_index(target, sizes))))
    return lax.ppermute(block, tuple(axes) if len(axes) > 1 else axes[0], pairs)


def along_y(block, d):
    return permute(block, ("y",), lambda y: ((y + d) % 4,))


def along_x(block, d):
    def route(xh, xl):
        x = (2 * xh + xl + d) % 4
        return (x // 2, x % 2)

    return permute(block, ("xh", "xl"), route)


def other_core(block):
    return permute(block, ("c",), lambda c: (1 - c,))


def in_vmem(block):
    return pltpu.with_memory_space_constraint(block, pltpu.VMEM)


def cost(flops, size):
    return pl.CostEstimate(flops=flops, bytes_accessed=size, transcendentals=0)


def modulation_of(t_index, w_mod):
    fraction = 1.0 - t_index[0].astype(F32) / STEPS
    following = fraction - 1.0 / STEPS
    sigma_now = 3.0 * fraction / (1.0 + 2.0 * fraction)
    sigma_next = 3.0 * following / (1.0 + 2.0 * following)
    half_width = w_mod.shape[0] // 2
    frequency = jnp.exp(-math.log(10000.0) * jnp.arange(half_width).astype(F32) / half_width)
    angles = 1000.0 * sigma_now * frequency
    embedding = jnp.concatenate([jnp.cos(angles), jnp.sin(angles)])
    time_features = jax.nn.silu(embedding).astype(BF)
    shifts = jnp.dot(time_features[None, :], w_mod, preferred_element_type=F32)[0]
    return (lax.optimization_barrier(shifts), sigma_next - sigma_now)


def padded_pieces(rows):
    pieces = rows.reshape(-1, PIECE, rows.shape[1])
    return jnp.pad(pieces, ((0, 0), (0, PADDED - PIECE), (0, 0)))


STATE_ROWS = 640


def total_lanes(total):
    hi = total.astype(BF).astype(F32)
    mid = (total - hi).astype(BF).astype(F32)
    low = total - hi - mid
    lane = lax.broadcasted_iota(jnp.int32, (DH, 16), 1)
    zero = jnp.zeros((DH, 16), F32)
    return jnp.where(lane == 0, hi, jnp.where(lane == 1, mid, jnp.where(lane == 2, low, zero))).astype(BF)


def state_kernel(k_ref, v_ref, decay_ref, cumulative_ref, packed_ref):
    decay = decay_ref[...]
    hi = decay.astype(BF)
    rest = decay - hi.astype(F32)
    mid = rest.astype(BF)
    low = (rest - mid.astype(F32)).astype(BF)
    row = lax.broadcasted_iota(jnp.int32, (TOKENS, TOKENS), 0)
    column = lax.broadcasted_iota(jnp.int32, (TOKENS, TOKENS), 1)
    triangle = jnp.where(row <= column, 1.0, 0.0).astype(BF)
    cumulative = sum(
        jnp.dot(part, triangle, preferred_element_type=F32) for part in (low, mid, hi)
    )
    cumulative_ref[...] = cumulative
    for h in range(HEADS):
        mine = cumulative[h : h + 1, :]
        total = mine[:, TOKENS - 1 :]
        heads = pl.ds(DH * h, DH)
        scaled = (k_ref[heads, :].astype(F32) * jnp.exp(total - mine)).astype(BF)
        state = lax.dot_general(
            v_ref[heads, :], scaled, (((1,), (1,)), ((), ())), preferred_element_type=F32
        )
        packed_ref[heads, 0:DH] = state.astype(BF)
        packed_ref[heads, DH:SHARE] = total_lanes(total)
    packed_ref[HEADS * DH :, :] = jnp.zeros((STATE_ROWS - HEADS * DH, SHARE), BF)


def own_state(keys, values, log_decay):
    return pl.pallas_call(
        state_kernel,
        out_shape=(
            jax.ShapeDtypeStruct((HEADS, TOKENS), F32),
            jax.ShapeDtypeStruct((STATE_ROWS, SHARE), BF),
        ),
        in_specs=[VMEM] * 3,
        out_specs=(VMEM, VMEM),
        cost_estimate=cost(10**9, 3 * 10**6),
    )(keys, values, log_decay)


def scan_kernel(blocks_ref, before_ref):
    state = jnp.zeros(before_ref.shape[1:], F32)
    for f in range(blocks_ref.shape[0]):
        before_ref[f] = state.astype(BF)
        packed = blocks_ref[f].astype(F32)
        total = jnp.sum(packed[:, DH : DH + 3], axis=1, keepdims=True)
        state = packed + jnp.exp(total) * state


def scan_blocks(blocks):
    return pl.pallas_call(
        scan_kernel,
        out_shape=jax.ShapeDtypeStruct(blocks.shape, BF),
        in_specs=[VMEM],
        out_specs=VMEM,
        cost_estimate=cost(10**6, 10**6),
    )(in_vmem(blocks))


def inner_kernel(q_ref, k_ref, v_ref, cumulative_ref, labels_ref, out_ref):
    cumulative = cumulative_ref[...]
    labels = labels_ref[...].astype(F32)
    stacked = jnp.concatenate([cumulative, labels, jnp.zeros((2, TOKENS), F32)], axis=0)
    columns = stacked.T
    visible = columns[:, HEADS : HEADS + 1] <= labels
    for h in range(HEADS):
        heads = pl.ds(DH * h, DH)
        scores = lax.dot_general(
            k_ref[heads, :], q_ref[heads, :], (((0,), (0,)), ((), ())), preferred_element_type=F32
        )
        decay = jnp.exp(jnp.minimum(cumulative[h : h + 1, :] - columns[:, h : h + 1], 0.0))
        weights = jnp.where(visible, decay * (DH**-0.5), 0.0)
        probs = (scores * weights).astype(BF)
        out_ref[heads, :] = jnp.dot(v_ref[heads, :], probs, preferred_element_type=F32)


def inner_part(queries, keys, values, cumulative, labels):
    return pl.pallas_call(
        inner_kernel,
        out_shape=jax.ShapeDtypeStruct((HEADS * DH, TOKENS), F32),
        in_specs=[VMEM] * 5,
        out_specs=VMEM,
        cost_estimate=cost(5 * 10**9, 4 * 10**6),
    )(queries, keys, values, cumulative, labels)


def mix_kernel(q_ref, inner_ref, cumulative_ref, before_ref, out_ref):
    for h in range(HEADS):
        heads = pl.ds(DH * h, DH)
        carried = jnp.dot(
            before_ref[heads, :][:, 0:DH], q_ref[heads, :], preferred_element_type=F32
        )
        numerator = inner_ref[heads, :] + carried * (
            jnp.exp(cumulative_ref[h : h + 1, :]) * (DH**-0.5)
        )
        mean = jnp.sum(numerator * numerator, axis=0, keepdims=True) * (1.0 / DH)
        out_ref[heads, :] = (numerator * lax.rsqrt(mean + 1e-06)).astype(BF)


def mix(queries, inner, cumulative, before):
    return pl.pallas_call(
        mix_kernel,
        out_shape=jax.ShapeDtypeStruct((HEADS * DH, TOKENS), BF),
        in_specs=[VMEM] * 4,
        out_specs=VMEM,
        cost_estimate=cost(10**8, 4 * 10**6),
    )(queries, inner, cumulative, in_vmem(before))


FARTHEST_FIRST = (2, 1, 3, 0)


def head_kernel(place_ref, mixed_ref, own_ref, first_ref, second_ref, *out_refs):
    for d, out_ref in zip(FARTHEST_FIRST, out_refs):
        start = pl.multiple_of(((place_ref[2] + d) % 4) * SHARE, SHARE)
        tokens = mixed_ref[:, pl.ds(start, SHARE)]
        row = 0
        for weight_ref in (own_ref, first_ref, second_ref):
            weight = weight_ref[...].reshape(-1, weight_ref.shape[2])
            rows = weight.shape[0]
            out_ref[row : row + rows, :] = jnp.dot(
                weight, tokens, preferred_element_type=F32
            ).astype(BF)
            row += rows


def head_terms(place, mixed, weights):
    return pl.pallas_call(
        head_kernel,
        out_shape=[jax.ShapeDtypeStruct((ROWS, SHARE), BF)] * 4,
        in_specs=[SMEM] + [VMEM] * 4,
        out_specs=[VMEM] * 4,
        cost_estimate=cost(2 * 10**9, 5 * 10**6),
    )(place, mixed, weights[0], *[in_vmem(w) for w in weights[1:]])


def piece_table(place_ref):
    c, xl = place_ref[0], place_ref[1]
    for hr in range(2):
        for z in range(8):
            for xr in range(2):
                h = c if hr == 0 else 1 - c
                x = xl if xr == 0 else 1 - xl
                yield hr * 16 + z * 2 + xr, 2 * (8 * x + z) + h, 16 * xr + 2 * z + h


def norm_kernel(place_ref, t0, t1, t2, t3, latent_ref, vector_ref, hidden_ref, normed_ref, work):
    sums = jnp.zeros((PADDED, SHARE), F32)
    for own, natural, term in piece_table(place_ref):
        attention = sum(t[term].astype(F32) for t in (t0, t1, t2, t3))
        hidden = latent_ref[natural].astype(F32) + vector_ref[natural][:, 3:4] * attention
        hidden_ref[own] = hidden
        sums = sums + hidden
    mean = jnp.sum(sums, axis=0, keepdims=True) * (1.0 / WIDTH)
    real = lax.broadcasted_iota(jnp.int32, (PADDED, SHARE), 0) < PIECE
    squares = jnp.zeros((PADDED, SHARE), F32)
    for own in range(PIECES):
        centered = hidden_ref[own] - mean
        squares = squares + centered * centered
    squares = jnp.where(real, squares, 0.0)
    scaling = lax.rsqrt(jnp.sum(squares, axis=0, keepdims=True) * (1.0 / WIDTH) + 1e-06)
    for own, natural, _ in piece_table(place_ref):
        vectors = vector_ref[natural]
        normed = (hidden_ref[own] - mean) * scaling * (1.0 + vectors[:, 1:2]) + vectors[:, 0:1]
        work[own * PADDED : (own + 1) * PADDED, :] = jnp.where(real, normed, 0.0)
    for i in range(ROWS // 256):
        normed_ref[:, 256 * i : 256 * (i + 1)] = work[256 * i : 256 * (i + 1), :].T.astype(BF)


def arrived(parts):
    pieces = [p.reshape(PIECES, PADDED, SHARE) for p in parts]
    return [in_vmem(p) for p in pieces[:-1]] + pieces[-1:]


def norm(place, terms, latents, vectors):
    return pl.pallas_call(
        norm_kernel,
        out_shape=(
            jax.ShapeDtypeStruct((PIECES, PADDED, SHARE), F32),
            jax.ShapeDtypeStruct((SHARE, ROWS), BF),
        ),
        in_specs=[SMEM] + [VMEM] * 6,
        out_specs=(VMEM, VMEM),
        scratch_shapes=[pltpu.VMEM((ROWS, SHARE), F32)],
        cost_estimate=cost(10**7, 8 * 10**6),
    )(place, *arrived(terms), latents, vectors)


def last_kernel(place_ref, step_ref, f0, f1, f2, f3, hidden_ref, latent_ref, vector_ref, v_ref, a_ref, v_work, a_work):
    step = step_ref[0]
    c, xl = place_ref[0], place_ref[1]
    for natural in range(PIECES):
        f, h = natural // 2, natural % 2
        hr = c if h == 0 else 1 - c
        xr = xl if f < 8 else 1 - xl
        own = hr * 16 + (f % 8) * 2 + xr
        feed = sum(f[own].astype(F32) for f in (f0, f1, f2, f3))
        velocity = (hidden_ref[own] + vector_ref[natural][:, 2:3] * feed).astype(BF).astype(F32)
        rows = slice(PIECE * natural, PIECE * (natural + 1))
        v_work[rows, :] = velocity[:PIECE]
        a_work[rows, :] = (latent_ref[natural].astype(F32) + step * velocity)[:PIECE]
    v_ref[...] = v_work[...].astype(BF)
    a_ref[...] = a_work[...].astype(BF)


def last(place, step_size, feeds, hidden, latents, vectors):
    shape = jax.ShapeDtypeStruct((WIDTH, SHARE), BF)
    return pl.pallas_call(
        last_kernel,
        out_shape=(shape, shape),
        in_specs=[SMEM] * 2 + [VMEM] * 7,
        out_specs=(VMEM, VMEM),
        scratch_shapes=[pltpu.VMEM((WIDTH, SHARE), F32)] * 2,
        cost_estimate=cost(10**7, 8 * 10**6),
    )(place, step_size, *arrived(feeds), hidden, latents, vectors)


HALF = ROWS // 2


def units_kernel(pieces, *refs):
    token_refs = refs[:pieces]
    own_ref, other_ref = refs[pieces : pieces + 2]
    out_refs = refs[pieces + 2 : -3]
    tokens, sums, units = refs[-3:]
    step = pl.program_id(0)

    def up(ref, first):
        weight = ref[...].reshape(HALF, -1)
        return jnp.dot(tokens[:, first : first + HALF], weight, preferred_element_type=F32)

    def down(ref):
        weight = ref[...].reshape(HALF, -1)
        feed = lax.dot_general(
            weight, units[...], (((1,), (1,)), ((), ())), preferred_element_type=F32
        ).astype(BF)
        for n, out_ref in enumerate(out_refs):
            out_ref[...] = feed[:, SHARE * n : SHARE * (n + 1)]

    @pl.when(step == 0)
    def _():
        row = 0
        for token_ref in token_refs:
            tokens[row : row + token_ref.shape[0], :] = token_ref[...]
            row += token_ref.shape[0]
        sums[...] = up(own_ref, 0)

    @pl.when(step == 1)
    def _():
        units[...] = jax.nn.gelu(sums[...] + up(other_ref, HALF), approximate=True).astype(BF)

    @pl.when(step == 2)
    def _():
        down(own_ref)

    @pl.when(step == 3)
    def _():
        down(other_ref)


def unit_terms(tokens, own, other):
    chunks = sum(t.shape[0] for t in tokens) // SHARE
    hidden_units = own.shape[4]
    block = (8, 2, 1, PADDED, hidden_units)
    return pl.pallas_call(
        functools.partial(units_kernel, len(tokens)),
        grid=(4,),
        out_shape=[jax.ShapeDtypeStruct((ROWS, SHARE), BF)] * chunks,
        in_specs=[pl.BlockSpec(t.shape, lambda i: (0, 0)) for t in tokens]
        + [
            pl.BlockSpec(block, lambda i: (0, 0, jnp.where(i >= 2, 1, 0), 0, 0)),
            pl.BlockSpec(block, lambda i: (0, 0, jnp.where(i >= 3, 1, 0), 0, 0)),
        ],
        out_specs=[pl.BlockSpec((HALF, SHARE), lambda i: (jnp.where(i >= 3, 1, 0), 0))] * chunks,
        scratch_shapes=[
            pltpu.VMEM((SHARE * chunks, ROWS), BF),
            pltpu.VMEM((SHARE * chunks, hidden_units), F32),
            pltpu.VMEM((SHARE * chunks, hidden_units), BF),
        ],
        cost_estimate=cost(4 * SHARE * chunks * ROWS * hidden_units, 4 * ROWS * hidden_units),
    )(*tokens, own, other)


def block(
    latents, queries, keys, values, log_decay, block_ids, t_index, w_mod, w_out, w_up, w_down
):
    y, c, xl = lax.axis_index("y"), lax.axis_index("c"), lax.axis_index("xl")
    place = jnp.stack([c, xl, y]).astype(jnp.int32)

    def core_half(both):
        return jnp.where(c == 0, both[..., 0, :, :], both[..., 1, :, :])

    out_mine = padded_pieces(w_out.T).reshape(2 * PADDED, -1)
    out_own = lax.all_gather(out_mine, "z", axis=0)
    out_weights = [out_own, along_x(out_own[:4], 1), along_x(out_own[4:], -1)]
    mine = core_half(jnp.stack([padded_pieces(w_up), padded_pieces(w_down.T)]))
    queries, keys, values = queries.T, keys.T, values.T
    cumulative, packed = own_state(keys, values, log_decay)
    slices = lax.all_to_all(packed.reshape(16, -1, SHARE), ("xl", "z"), 0, 0)
    mine, _ = lax.optimization_barrier((mine, slices))
    mine_x = along_x(mine, 1)
    ahead = scan_blocks(slices)
    before = lax.all_to_all(ahead, ("xl", "z"), 0, 0).reshape(STATE_ROWS, SHARE)
    mine, mine_x, _ = lax.optimization_barrier((mine, mine_x, before))
    half = lax.all_gather(jnp.stack([mine, mine_x]), "z", axis=0)
    inner = inner_part(queries, keys, values, cumulative, block_ids[None, :])
    mixed = mix(queries, inner, cumulative, before)

    parts = head_terms(place, mixed, out_weights)
    terms = [along_y(parts[i], d) for i, d in enumerate(FARTHEST_FIRST[:3])] + [parts[3]]

    shifts, step_size = modulation_of(t_index, w_mod)
    vectors = padded_pieces(shifts.reshape(4, WIDTH).T)
    latent_pieces = padded_pieces(latents.T)
    hidden, normed = norm(place, terms, latent_pieces, vectors)

    above, below = along_y(normed, -1), along_y(normed, 1)
    far = [along_y(above[: SHARE // 2], -1), along_y(below[SHARE // 2 :], 1)]
    half, _ = lax.optimization_barrier((half, normed))
    other = other_core(half)
    near = unit_terms([above, below], half, other)
    feeds = []
    for d, part in zip((1, 3), near):
        feeds.append(along_y(part, d))
    normed, _ = lax.optimization_barrier((normed, near[0]))
    rest = unit_terms([normed] + far, half, other)
    feeds += [along_y(rest[1], 2), rest[0]]
    step = step_size[None] if step_size.ndim == 0 else step_size
    velocity, advanced = last(place, step, feeds, hidden, latent_pieces, vectors)
    return (velocity.T, advanced.T)


def solution(mesh):
    fine = Mesh(mesh.devices.reshape(tuple(AXES.values())), tuple(AXES))
    pool, frame = ("xh", "c"), ("xl", "z")
    rows = P(pool + frame + ("y",), None)
    return jax.shard_map(
        block,
        mesh=fine,
        in_specs=(
            rows,
            P(pool + frame, "y"),
            P(pool + frame, "y"),
            P(pool + frame, "y"),
            P("y", pool + frame),
            P(pool + frame),
            P(pool),
            P(),
            P("y", frame),
            P(frame, "y"),
            P("y", frame),
        ),
        out_specs=(rows, rows),
        check_vma=False,
    )
```

```python
import functools
import math

import jax
import jax.numpy as jnp
import numpy as np
from jax import lax
from jax.experimental import pallas as pl
from jax.experimental.pallas import tpu as pltpu
from jax.sharding import Mesh, PartitionSpec as P


STEPS = 50
BF = jnp.bfloat16
F32 = jnp.float32
AXES = {"xh": 2, "c": 2, "xl": 2, "z": 8, "y": 4}
HEADS = 5
DH = 112
TOKENS = 512
SHARE = 128
WIDTH = 2240
PIECE = 70
PADDED = 72
PIECES = 32
ROWS = PIECES * PADDED
VMEM = pl.BlockSpec(memory_space=pltpu.VMEM)
SMEM = pl.BlockSpec(memory_space=pltpu.SMEM)


def permute(block, axes, route):
    sizes = [AXES[a] for a in axes]
    pairs = []
    for i in range(int(np.prod(sizes))):
        target = route(*[int(v) for v in np.unravel_index(i, sizes)])
        if target is not None:
            pairs.append((i, int(np.ravel_multi_index(target, sizes))))
    return lax.ppermute(block, tuple(axes) if len(axes) > 1 else axes[0], pairs)


def along_y(block, d):
    return permute(block, ("y",), lambda y: ((y + d) % 4,))


def along_x(block, d):
    def route(xh, xl):
        x = (2 * xh + xl + d) % 4
        return (x // 2, x % 2)

    return permute(block, ("xh", "xl"), route)


def other_core(block):
    return permute(block, ("c",), lambda c: (1 - c,))


def in_vmem(block):
    return pltpu.with_memory_space_constraint(block, pltpu.VMEM)


def cost(flops, size):
    return pl.CostEstimate(flops=flops, bytes_accessed=size, transcendentals=0)


def modulation_of(t_index, w_mod):
    fraction = 1.0 - t_index[0].astype(F32) / STEPS
    following = fraction - 1.0 / STEPS
    sigma_now = 3.0 * fraction / (1.0 + 2.0 * fraction)
    sigma_next = 3.0 * following / (1.0 + 2.0 * following)
    half_width = w_mod.shape[0] // 2
    frequency = jnp.exp(-math.log(10000.0) * jnp.arange(half_width).astype(F32) / half_width)
    angles = 1000.0 * sigma_now * frequency
    embedding = jnp.concatenate([jnp.cos(angles), jnp.sin(angles)])
    time_features = jax.nn.silu(embedding).astype(BF)
    shifts = jnp.dot(time_features[None, :], w_mod, preferred_element_type=F32)[0]
    return (lax.optimization_barrier(shifts), sigma_next - sigma_now)


def padded_pieces(rows):
    pieces = rows.reshape(-1, PIECE, rows.shape[1])
    return jnp.pad(pieces, ((0, 0), (0, PADDED - PIECE), (0, 0)))


STATE_ROWS = 640


def total_lanes(total):
    hi = total.astype(BF).astype(F32)
    mid = (total - hi).astype(BF).astype(F32)
    low = total - hi - mid
    lane = lax.broadcasted_iota(jnp.int32, (DH, 16), 1)
    zero = jnp.zeros((DH, 16), F32)
    return jnp.where(lane == 0, hi, jnp.where(lane == 1, mid, jnp.where(lane == 2, low, zero))).astype(BF)


def state_kernel(k_ref, v_ref, decay_ref, cumulative_ref, packed_ref):
    decay = decay_ref[...]
    hi = decay.astype(BF)
    rest = decay - hi.astype(F32)
    mid = rest.astype(BF)
    low = (rest - mid.astype(F32)).astype(BF)
    row = lax.broadcasted_iota(jnp.int32, (TOKENS, TOKENS), 0)
    column = lax.broadcasted_iota(jnp.int32, (TOKENS, TOKENS), 1)
    triangle = jnp.where(row <= column, 1.0, 0.0).astype(BF)
    cumulative = sum(
        jnp.dot(part, triangle, preferred_element_type=F32) for part in (low, mid, hi)
    )
    cumulative_ref[...] = cumulative
    for h in range(HEADS):
        mine = cumulative[h : h + 1, :]
        total = mine[:, TOKENS - 1 :]
        heads = pl.ds(DH * h, DH)
        scaled = (k_ref[heads, :].astype(F32) * jnp.exp(total - mine)).astype(BF)
        state = lax.dot_general(
            v_ref[heads, :], scaled, (((1,), (1,)), ((), ())), preferred_element_type=F32
        )
        packed_ref[heads, 0:DH] = state.astype(BF)
        packed_ref[heads, DH:SHARE] = total_lanes(total)
    packed_ref[HEADS * DH :, :] = jnp.zeros((STATE_ROWS - HEADS * DH, SHARE), BF)


def own_state(keys, values, log_decay):
    return pl.pallas_call(
        state_kernel,
        out_shape=(
            jax.ShapeDtypeStruct((HEADS, TOKENS), F32),
            jax.ShapeDtypeStruct((STATE_ROWS, SHARE), BF),
        ),
        in_specs=[VMEM] * 3,
        out_specs=(VMEM, VMEM),
        cost_estimate=cost(10**9, 3 * 10**6),
    )(keys, values, log_decay)


def scan_kernel(blocks_ref, before_ref):
    state = jnp.zeros(before_ref.shape[1:], F32)
    for f in range(blocks_ref.shape[0]):
        before_ref[f] = state.astype(BF)
        packed = blocks_ref[f].astype(F32)
        total = jnp.sum(packed[:, DH : DH + 3], axis=1, keepdims=True)
        state = packed + jnp.exp(total) * state


def scan_blocks(blocks):
    return pl.pallas_call(
        scan_kernel,
        out_shape=jax.ShapeDtypeStruct(blocks.shape, BF),
        in_specs=[VMEM],
        out_specs=VMEM,
        cost_estimate=cost(10**6, 10**6),
    )(in_vmem(blocks))


def inner_kernel(q_ref, k_ref, v_ref, cumulative_ref, labels_ref, out_ref):
    cumulative = cumulative_ref[...]
    labels = labels_ref[...].astype(F32)
    stacked = jnp.concatenate([cumulative, labels, jnp.zeros((2, TOKENS), F32)], axis=0)
    columns = stacked.T
    visible = columns[:, HEADS : HEADS + 1] <= labels
    for h in range(HEADS):
        heads = pl.ds(DH * h, DH)
        scores = lax.dot_general(
            k_ref[heads, :], q_ref[heads, :], (((0,), (0,)), ((), ())), preferred_element_type=F32
        )
        decay = jnp.exp(jnp.minimum(cumulative[h : h + 1, :] - columns[:, h : h + 1], 0.0))
        weights = jnp.where(visible, decay * (DH**-0.5), 0.0)
        probs = (scores * weights).astype(BF)
        out_ref[heads, :] = jnp.dot(v_ref[heads, :], probs, preferred_element_type=F32)


def inner_part(queries, keys, values, cumulative, labels):
    return pl.pallas_call(
        inner_kernel,
        out_shape=jax.ShapeDtypeStruct((HEADS * DH, TOKENS), F32),
        in_specs=[VMEM] * 5,
        out_specs=VMEM,
        cost_estimate=cost(5 * 10**9, 4 * 10**6),
    )(queries, keys, values, cumulative, labels)


def mix_kernel(q_ref, inner_ref, cumulative_ref, before_ref, out_ref):
    for h in range(HEADS):
        heads = pl.ds(DH * h, DH)
        carried = jnp.dot(
            before_ref[heads, :][:, 0:DH], q_ref[heads, :], preferred_element_type=F32
        )
        numerator = inner_ref[heads, :] + carried * (
            jnp.exp(cumulative_ref[h : h + 1, :]) * (DH**-0.5)
        )
        mean = jnp.sum(numerator * numerator, axis=0, keepdims=True) * (1.0 / DH)
        out_ref[heads, :] = (numerator * lax.rsqrt(mean + 1e-06)).astype(BF)


def mix(queries, inner, cumulative, before):
    return pl.pallas_call(
        mix_kernel,
        out_shape=jax.ShapeDtypeStruct((HEADS * DH, TOKENS), BF),
        in_specs=[VMEM] * 4,
        out_specs=VMEM,
        cost_estimate=cost(10**8, 4 * 10**6),
    )(queries, inner, cumulative, in_vmem(before))


FARTHEST_FIRST = (2, 1, 3, 0)


def head_kernel(place_ref, mixed_ref, own_ref, first_ref, second_ref, *out_refs):
    for d, out_ref in zip(FARTHEST_FIRST, out_refs):
        start = pl.multiple_of(((place_ref[2] + d) % 4) * SHARE, SHARE)
        tokens = mixed_ref[:, pl.ds(start, SHARE)]
        row = 0
        for weight_ref in (own_ref, first_ref, second_ref):
            weight = weight_ref[...].reshape(-1, weight_ref.shape[2])
            rows = weight.shape[0]
            out_ref[row : row + rows, :] = jnp.dot(
                weight, tokens, preferred_element_type=F32
            ).astype(BF)
            row += rows


def head_terms(place, mixed, weights):
    return pl.pallas_call(
        head_kernel,
        out_shape=[jax.ShapeDtypeStruct((ROWS, SHARE), BF)] * 4,
        in_specs=[SMEM] + [VMEM] * 4,
        out_specs=[VMEM] * 4,
        cost_estimate=cost(2 * 10**9, 5 * 10**6),
    )(place, mixed, weights[0], *[in_vmem(w) for w in weights[1:]])


def piece_table(place_ref):
    c, xl = place_ref[0], place_ref[1]
    for hr in range(2):
        for z in range(8):
            for xr in range(2):
                h = c if hr == 0 else 1 - c
                x = xl if xr == 0 else 1 - xl
                yield hr * 16 + z * 2 + xr, 2 * (8 * x + z) + h, 16 * xr + 2 * z + h


def norm_kernel(place_ref, t0, t1, t2, t3, latent_ref, vector_ref, hidden_ref, normed_ref, work):
    sums = jnp.zeros((PADDED, SHARE), F32)
    for own, natural, term in piece_table(place_ref):
        attention = sum(t[term].astype(F32) for t in (t0, t1, t2, t3))
        hidden = latent_ref[natural].astype(F32) + vector_ref[natural][:, 3:4] * attention
        hidden_ref[own] = hidden
        sums = sums + hidden
    mean = jnp.sum(sums, axis=0, keepdims=True) * (1.0 / WIDTH)
    real = lax.broadcasted_iota(jnp.int32, (PADDED, SHARE), 0) < PIECE
    squares = jnp.zeros((PADDED, SHARE), F32)
    for own in range(PIECES):
        centered = hidden_ref[own] - mean
        squares = squares + centered * centered
    squares = jnp.where(real, squares, 0.0)
    scaling = lax.rsqrt(jnp.sum(squares, axis=0, keepdims=True) * (1.0 / WIDTH) + 1e-06)
    for own, natural, _ in piece_table(place_ref):
        vectors = vector_ref[natural]
        normed = (hidden_ref[own] - mean) * scaling * (1.0 + vectors[:, 1:2]) + vectors[:, 0:1]
        work[own * PADDED : (own + 1) * PADDED, :] = jnp.where(real, normed, 0.0)
    for i in range(ROWS // 256):
        normed_ref[:, 256 * i : 256 * (i + 1)] = work[256 * i : 256 * (i + 1), :].T.astype(BF)


def arrived(parts):
    pieces = [p.reshape(PIECES, PADDED, SHARE) for p in parts]
    return [in_vmem(p) for p in pieces[:-1]] + pieces[-1:]


def norm(place, terms, latents, vectors):
    return pl.pallas_call(
        norm_kernel,
        out_shape=(
            jax.ShapeDtypeStruct((PIECES, PADDED, SHARE), F32),
            jax.ShapeDtypeStruct((SHARE, ROWS), BF),
        ),
        in_specs=[SMEM] + [VMEM] * 6,
        out_specs=(VMEM, VMEM),
        scratch_shapes=[pltpu.VMEM((ROWS, SHARE), F32)],
        cost_estimate=cost(10**7, 8 * 10**6),
    )(place, *arrived(terms), latents, vectors)


def last_kernel(place_ref, step_ref, f0, f1, f2, f3, hidden_ref, latent_ref, vector_ref, v_ref, a_ref, v_work, a_work):
    step = step_ref[0]
    c, xl = place_ref[0], place_ref[1]
    for natural in range(PIECES):
        f, h = natural // 2, natural % 2
        hr = c if h == 0 else 1 - c
        xr = xl if f < 8 else 1 - xl
        own = hr * 16 + (f % 8) * 2 + xr
        feed = sum(f[own].astype(F32) for f in (f0, f1, f2, f3))
        velocity = (hidden_ref[own] + vector_ref[natural][:, 2:3] * feed).astype(BF).astype(F32)
        rows = slice(PIECE * natural, PIECE * (natural + 1))
        v_work[rows, :] = velocity[:PIECE]
        a_work[rows, :] = (latent_ref[natural].astype(F32) + step * velocity)[:PIECE]
    v_ref[...] = v_work[...].astype(BF)
    a_ref[...] = a_work[...].astype(BF)


def last(place, step_size, feeds, hidden, latents, vectors):
    shape = jax.ShapeDtypeStruct((WIDTH, SHARE), BF)
    return pl.pallas_call(
        last_kernel,
        out_shape=(shape, shape),
        in_specs=[SMEM] * 2 + [VMEM] * 7,
        out_specs=(VMEM, VMEM),
        scratch_shapes=[pltpu.VMEM((WIDTH, SHARE), F32)] * 2,
        cost_estimate=cost(10**7, 8 * 10**6),
    )(place, step_size, *arrived(feeds), hidden, latents, vectors)


HALF = ROWS // 2


def units_kernel(pieces, *refs):
    token_refs = refs[:pieces]
    own_ref, other_ref = refs[pieces : pieces + 2]
    out_refs = refs[pieces + 2 : -4]
    tokens, units, own, arrived_sems = refs[-4:]
    copies = [
        pltpu.make_async_copy(own_ref.at[:, :, w], own.at[w], arrived_sems.at[w]) for w in range(2)
    ]
    for copy in copies:
        copy.start()
    row = 0
    for token_ref in token_refs:
        tokens[row : row + token_ref.shape[0], :] = token_ref[...]
        row += token_ref.shape[0]

    def up(weight, first):
        weight = weight.reshape(HALF, -1)
        return jnp.dot(tokens[:, first : first + HALF], weight, preferred_element_type=F32)

    def down(weight, first):
        feed = lax.dot_general(
            weight.reshape(HALF, -1),
            units[...],
            (((1,), (1,)), ((), ())),
            preferred_element_type=F32,
        ).astype(BF)
        for n, out_ref in enumerate(out_refs):
            out_ref[first : first + HALF, :] = feed[:, SHARE * n : SHARE * (n + 1)]

    sums = up(other_ref[:, :, 0], HALF)
    copies[0].wait()
    sums = sums + up(own[0], 0)
    units[...] = jax.nn.gelu(sums, approximate=True).astype(BF)
    down(other_ref[:, :, 1], HALF)
    copies[1].wait()
    down(own[1], 0)


def unit_terms(tokens, own, other):
    chunks = sum(t.shape[0] for t in tokens) // SHARE
    hidden_units = own.shape[4]
    return pl.pallas_call(
        functools.partial(units_kernel, len(tokens)),
        out_shape=[jax.ShapeDtypeStruct((ROWS, SHARE), BF)] * chunks,
        in_specs=[VMEM] * len(tokens) + [pl.BlockSpec(memory_space=pltpu.HBM), VMEM],
        out_specs=[VMEM] * chunks,
        scratch_shapes=[
            pltpu.VMEM((SHARE * chunks, ROWS), BF),
            pltpu.VMEM((SHARE * chunks, hidden_units), BF),
            pltpu.VMEM((2, 8, 2, PADDED, hidden_units), BF),
            pltpu.SemaphoreType.DMA((2,)),
        ],
        compiler_params=pltpu.CompilerParams(vmem_limit_bytes=28 << 20),
        cost_estimate=cost(4 * SHARE * chunks * ROWS * hidden_units, 4 * ROWS * hidden_units),
    )(*tokens, own, other)


def block(
    latents, queries, keys, values, log_decay, block_ids, t_index, w_mod, w_out, w_up, w_down
):
    y, c, xl = lax.axis_index("y"), lax.axis_index("c"), lax.axis_index("xl")
    place = jnp.stack([c, xl, y]).astype(jnp.int32)

    def core_half(both):
        return jnp.where(c == 0, both[..., 0, :, :], both[..., 1, :, :])

    out_mine = padded_pieces(w_out.T).reshape(2 * PADDED, -1)
    out_own = lax.all_gather(out_mine, "z", axis=0)
    out_weights = [out_own, along_x(out_own[:4], 1), along_x(out_own[4:], -1)]
    mine = core_half(jnp.stack([padded_pieces(w_up), padded_pieces(w_down.T)]))
    queries, keys, values = queries.T, keys.T, values.T
    cumulative, packed = own_state(keys, values, log_decay)
    slices = lax.all_to_all(packed.reshape(16, -1, SHARE), ("xl", "z"), 0, 0)
    mine, _ = lax.optimization_barrier((mine, slices))
    mine_x = along_x(mine, 1)
    ahead = scan_blocks(slices)
    before = lax.all_to_all(ahead, ("xl", "z"), 0, 0).reshape(STATE_ROWS, SHARE)
    mine, mine_x, _ = lax.optimization_barrier((mine, mine_x, before))
    half = lax.all_gather(jnp.stack([mine, mine_x]), "z", axis=0)
    inner = inner_part(queries, keys, values, cumulative, block_ids[None, :])
    mixed = mix(queries, inner, cumulative, before)

    parts = head_terms(place, mixed, out_weights)
    terms = [along_y(parts[i], d) for i, d in enumerate(FARTHEST_FIRST[:3])] + [parts[3]]

    shifts, step_size = modulation_of(t_index, w_mod)
    vectors = padded_pieces(shifts.reshape(4, WIDTH).T)
    latent_pieces = padded_pieces(latents.T)
    hidden, normed = norm(place, terms, latent_pieces, vectors)

    above, below = along_y(normed, -1), along_y(normed, 1)
    far = [along_y(above[: SHARE // 2], -1), along_y(below[SHARE // 2 :], 1)]
    half, _ = lax.optimization_barrier((half, normed))
    weights = [half, in_vmem(other_core(half))]
    near = unit_terms([in_vmem(above), in_vmem(below)], *weights)
    feeds = []
    for d, part in zip((1, 3), near):
        feeds.append(along_y(part, d))
    normed, _ = lax.optimization_barrier((normed, near[0]))
    rest = unit_terms([normed] + [in_vmem(f) for f in far], *weights)
    feeds += [along_y(rest[1], 2), rest[0]]
    step = step_size[None] if step_size.ndim == 0 else step_size
    velocity, advanced = last(place, step, feeds, hidden, latent_pieces, vectors)
    return (velocity.T, advanced.T)


def solution(mesh):
    fine = Mesh(mesh.devices.reshape(tuple(AXES.values())), tuple(AXES))
    pool, frame = ("xh", "c"), ("xl", "z")
    rows = P(pool + frame + ("y",), None)
    return jax.shard_map(
        block,
        mesh=fine,
        in_specs=(
            rows,
            P(pool + frame, "y"),
            P(pool + frame, "y"),
            P(pool + frame, "y"),
            P("y", pool + frame),
            P(pool + frame),
            P(pool),
            P(),
            P("y", frame),
            P(frame, "y"),
            P("y", frame),
        ),
        out_specs=(rows, rows),
        check_vma=False,
    )
```

```python
import functools
import math

import jax
import jax.numpy as jnp
import numpy as np
from jax import lax
from jax.experimental import pallas as pl
from jax.experimental.pallas import tpu as pltpu
from jax.sharding import Mesh, PartitionSpec as P


STEPS = 50
BF = jnp.bfloat16
F32 = jnp.float32
AXES = {"xh": 2, "c": 2, "xl": 2, "z": 8, "y": 4}
HEADS = 5
DH = 112
TOKENS = 512
SHARE = 128
WIDTH = 2240
PIECE = 70
PADDED = 72
PIECES = 32
ROWS = PIECES * PADDED
VMEM = pl.BlockSpec(memory_space=pltpu.VMEM)
SMEM = pl.BlockSpec(memory_space=pltpu.SMEM)
SMALL = pltpu.CompilerParams(vmem_limit_bytes=56 << 20)


def permute(block, axes, route):
    sizes = [AXES[a] for a in axes]
    pairs = []
    for i in range(int(np.prod(sizes))):
        target = route(*[int(v) for v in np.unravel_index(i, sizes)])
        if target is not None:
            pairs.append((i, int(np.ravel_multi_index(target, sizes))))
    return lax.ppermute(block, tuple(axes) if len(axes) > 1 else axes[0], pairs)


def along_y(block, d):
    return permute(block, ("y",), lambda y: ((y + d) % 4,))


def along_x(block, d):
    def route(xh, xl):
        x = (2 * xh + xl + d) % 4
        return (x // 2, x % 2)

    return permute(block, ("xh", "xl"), route)


def other_core(block):
    return permute(block, ("c",), lambda c: (1 - c,))


def in_vmem(block):
    return pltpu.with_memory_space_constraint(block, pltpu.VMEM)


def cost(flops, size):
    return pl.CostEstimate(flops=flops, bytes_accessed=size, transcendentals=0)


def modulation_of(t_index, w_mod):
    fraction = 1.0 - t_index[0].astype(F32) / STEPS
    following = fraction - 1.0 / STEPS
    sigma_now = 3.0 * fraction / (1.0 + 2.0 * fraction)
    sigma_next = 3.0 * following / (1.0 + 2.0 * following)
    half_width = w_mod.shape[0] // 2
    frequency = jnp.exp(-math.log(10000.0) * jnp.arange(half_width).astype(F32) / half_width)
    angles = 1000.0 * sigma_now * frequency
    embedding = jnp.concatenate([jnp.cos(angles), jnp.sin(angles)])
    time_features = jax.nn.silu(embedding).astype(BF)
    shifts = jnp.dot(time_features[None, :], w_mod, preferred_element_type=F32)[0]
    return (lax.optimization_barrier(shifts), sigma_next - sigma_now)


def padded_pieces(rows):
    pieces = rows.reshape(-1, PIECE, rows.shape[1])
    return jnp.pad(pieces, ((0, 0), (0, PADDED - PIECE), (0, 0)))


STATE_ROWS = 640


def total_lanes(total):
    hi = total.astype(BF).astype(F32)
    mid = (total - hi).astype(BF).astype(F32)
    low = total - hi - mid
    lane = lax.broadcasted_iota(jnp.int32, (DH, 16), 1)
    zero = jnp.zeros((DH, 16), F32)
    return jnp.where(lane == 0, hi, jnp.where(lane == 1, mid, jnp.where(lane == 2, low, zero))).astype(BF)


def state_kernel(k_ref, v_ref, decay_ref, cumulative_ref, packed_ref):
    decay = decay_ref[...]
    hi = decay.astype(BF)
    rest = decay - hi.astype(F32)
    mid = rest.astype(BF)
    low = (rest - mid.astype(F32)).astype(BF)
    row = lax.broadcasted_iota(jnp.int32, (TOKENS, TOKENS), 0)
    column = lax.broadcasted_iota(jnp.int32, (TOKENS, TOKENS), 1)
    triangle = jnp.where(row <= column, 1.0, 0.0).astype(BF)
    cumulative = sum(
        jnp.dot(part, triangle, preferred_element_type=F32) for part in (low, mid, hi)
    )
    cumulative_ref[...] = cumulative
    for h in range(HEADS):
        mine = cumulative[h : h + 1, :]
        total = mine[:, TOKENS - 1 :]
        heads = pl.ds(DH * h, DH)
        scaled = (k_ref[heads, :].astype(F32) * jnp.exp(total - mine)).astype(BF)
        state = lax.dot_general(
            v_ref[heads, :], scaled, (((1,), (1,)), ((), ())), preferred_element_type=F32
        )
        packed_ref[heads, 0:DH] = state.astype(BF)
        packed_ref[heads, DH:SHARE] = total_lanes(total)
    packed_ref[HEADS * DH :, :] = jnp.zeros((STATE_ROWS - HEADS * DH, SHARE), BF)


def own_state(keys, values, log_decay):
    return pl.pallas_call(
        state_kernel,
        out_shape=(
            jax.ShapeDtypeStruct((HEADS, TOKENS), F32),
            jax.ShapeDtypeStruct((STATE_ROWS, SHARE), BF),
        ),
        in_specs=[VMEM] * 3,
        out_specs=(VMEM, VMEM),
        cost_estimate=cost(10**9, 3 * 10**6),
    )(keys, values, log_decay)


def scan_kernel(blocks_ref, before_ref):
    state = jnp.zeros(before_ref.shape[1:], F32)
    for f in range(blocks_ref.shape[0]):
        before_ref[f] = state.astype(BF)
        packed = blocks_ref[f].astype(F32)
        total = jnp.sum(packed[:, DH : DH + 3], axis=1, keepdims=True)
        state = packed + jnp.exp(total) * state


def scan_blocks(blocks):
    return pl.pallas_call(
        scan_kernel,
        out_shape=jax.ShapeDtypeStruct(blocks.shape, BF),
        in_specs=[VMEM],
        out_specs=VMEM,
        cost_estimate=cost(10**6, 10**6),
    )(in_vmem(blocks))


def inner_kernel(q_ref, k_ref, v_ref, cumulative_ref, labels_ref, out_ref):
    cumulative = cumulative_ref[...]
    labels = labels_ref[...].astype(F32)
    stacked = jnp.concatenate([cumulative, labels, jnp.zeros((2, TOKENS), F32)], axis=0)
    columns = stacked.T
    visible = columns[:, HEADS : HEADS + 1] <= labels
    for h in range(HEADS):
        heads = pl.ds(DH * h, DH)
        scores = lax.dot_general(
            k_ref[heads, :], q_ref[heads, :], (((0,), (0,)), ((), ())), preferred_element_type=F32
        )
        decay = jnp.exp(jnp.minimum(cumulative[h : h + 1, :] - columns[:, h : h + 1], 0.0))
        weights = jnp.where(visible, decay * (DH**-0.5), 0.0)
        probs = (scores * weights).astype(BF)
        out_ref[heads, :] = jnp.dot(v_ref[heads, :], probs, preferred_element_type=F32)


def inner_part(queries, keys, values, cumulative, labels):
    return pl.pallas_call(
        inner_kernel,
        out_shape=jax.ShapeDtypeStruct((HEADS * DH, TOKENS), F32),
        in_specs=[VMEM] * 5,
        out_specs=VMEM,
        cost_estimate=cost(5 * 10**9, 4 * 10**6),
    )(queries, keys, values, cumulative, labels)


def mix_kernel(q_ref, inner_ref, cumulative_ref, before_ref, out_ref):
    for h in range(HEADS):
        heads = pl.ds(DH * h, DH)
        carried = jnp.dot(
            before_ref[heads, :][:, 0:DH], q_ref[heads, :], preferred_element_type=F32
        )
        numerator = inner_ref[heads, :] + carried * (
            jnp.exp(cumulative_ref[h : h + 1, :]) * (DH**-0.5)
        )
        mean = jnp.sum(numerator * numerator, axis=0, keepdims=True) * (1.0 / DH)
        out_ref[heads, :] = (numerator * lax.rsqrt(mean + 1e-06)).astype(BF)


def mix(queries, inner, cumulative, before):
    return pl.pallas_call(
        mix_kernel,
        out_shape=jax.ShapeDtypeStruct((HEADS * DH, TOKENS), BF),
        in_specs=[VMEM] * 4,
        out_specs=VMEM,
        cost_estimate=cost(10**8, 4 * 10**6),
    )(queries, inner, cumulative, in_vmem(before))


def head_kernel(distances, place_ref, mixed_ref, own_ref, first_ref, second_ref, *out_refs):
    for d, out_ref in zip(distances, out_refs):
        start = pl.multiple_of(((place_ref[2] + d) % 4) * SHARE, SHARE)
        tokens = mixed_ref[:, pl.ds(start, SHARE)]
        row = 0
        for weight_ref in (own_ref, first_ref, second_ref):
            weight = weight_ref[...].reshape(-1, weight_ref.shape[2])
            rows = weight.shape[0]
            out_ref[row : row + rows, :] = jnp.dot(
                weight, tokens, preferred_element_type=F32
            ).astype(BF)
            row += rows


def head_terms(distances, place, mixed, weights):
    return pl.pallas_call(
        functools.partial(head_kernel, distances),
        out_shape=[jax.ShapeDtypeStruct((ROWS, SHARE), BF)] * len(distances),
        in_specs=[SMEM] + [VMEM] * 4,
        out_specs=[VMEM] * len(distances),
        cost_estimate=cost(10**9, 4 * 10**6),
        compiler_params=SMALL,
    )(place, mixed, *weights)


def piece_table(place_ref):
    c, xl = place_ref[0], place_ref[1]
    for hr in range(2):
        for z in range(8):
            for xr in range(2):
                h = c if hr == 0 else 1 - c
                x = xl if xr == 0 else 1 - xl
                yield hr * 16 + z * 2 + xr, 2 * (8 * x + z) + h, 16 * xr + 2 * z + h


def norm_kernel(place_ref, t0, t1, t2, t3, latent_ref, vector_ref, hidden_ref, normed_ref, work):
    sums = jnp.zeros((PADDED, SHARE), F32)
    for own, natural, term in piece_table(place_ref):
        attention = sum(t[term].astype(F32) for t in (t0, t1, t2, t3))
        hidden = latent_ref[natural].astype(F32) + vector_ref[natural][:, 3:4] * attention
        hidden_ref[own] = hidden
        sums = sums + hidden
    mean = jnp.sum(sums, axis=0, keepdims=True) * (1.0 / WIDTH)
    real = lax.broadcasted_iota(jnp.int32, (PADDED, SHARE), 0) < PIECE
    squares = jnp.zeros((PADDED, SHARE), F32)
    for own in range(PIECES):
        centered = hidden_ref[own] - mean
        squares = squares + centered * centered
    squares = jnp.where(real, squares, 0.0)
    scaling = lax.rsqrt(jnp.sum(squares, axis=0, keepdims=True) * (1.0 / WIDTH) + 1e-06)
    for own, natural, _ in piece_table(place_ref):
        vectors = vector_ref[natural]
        normed = (hidden_ref[own] - mean) * scaling * (1.0 + vectors[:, 1:2]) + vectors[:, 0:1]
        work[own * PADDED : (own + 1) * PADDED, :] = jnp.where(real, normed, 0.0)
    for i in range(ROWS // 256):
        normed_ref[:, 256 * i : 256 * (i + 1)] = work[256 * i : 256 * (i + 1), :].T.astype(BF)


def arrived(parts):
    pieces = [p.reshape(PIECES, PADDED, SHARE) for p in parts]
    return [in_vmem(p) for p in pieces[:-1]] + pieces[-1:]


def norm(place, terms, latents, vectors):
    return pl.pallas_call(
        norm_kernel,
        out_shape=(
            jax.ShapeDtypeStruct((PIECES, PADDED, SHARE), F32),
            jax.ShapeDtypeStruct((SHARE, ROWS), BF),
        ),
        in_specs=[SMEM] + [VMEM] * 6,
        out_specs=(VMEM, VMEM),
        scratch_shapes=[pltpu.VMEM((ROWS, SHARE), F32)],
        cost_estimate=cost(10**7, 8 * 10**6),
        compiler_params=SMALL,
    )(place, *arrived(terms), latents, vectors)


def last_kernel(place_ref, step_ref, f0, f1, f2, f3, hidden_ref, latent_ref, vector_ref, v_ref, a_ref, v_work, a_work):
    step = step_ref[0]
    c, xl = place_ref[0], place_ref[1]
    for natural in range(PIECES):
        f, h = natural // 2, natural % 2
        hr = c if h == 0 else 1 - c
        xr = xl if f < 8 else 1 - xl
        own = hr * 16 + (f % 8) * 2 + xr
        feed = sum(f[own].astype(F32) for f in (f0, f1, f2, f3))
        velocity = (hidden_ref[own] + vector_ref[natural][:, 2:3] * feed).astype(BF).astype(F32)
        rows = slice(PIECE * natural, PIECE * (natural + 1))
        v_work[rows, :] = velocity[:PIECE]
        a_work[rows, :] = (latent_ref[natural].astype(F32) + step * velocity)[:PIECE]
    v_ref[...] = v_work[...].astype(BF)
    a_ref[...] = a_work[...].astype(BF)


def last(place, step_size, feeds, hidden, latents, vectors):
    shape = jax.ShapeDtypeStruct((WIDTH, SHARE), BF)
    return pl.pallas_call(
        last_kernel,
        out_shape=(shape, shape),
        in_specs=[SMEM] * 2 + [VMEM] * 7,
        out_specs=(VMEM, VMEM),
        scratch_shapes=[pltpu.VMEM((WIDTH, SHARE), F32)] * 2,
        cost_estimate=cost(10**7, 8 * 10**6),
        compiler_params=SMALL,
    )(place, step_size, *arrived(feeds), hidden, latents, vectors)


HALF = ROWS // 2


def units_kernel(pieces, *refs):
    token_refs = refs[:pieces]
    own_ref, other_ref = refs[pieces : pieces + 2]
    out_refs = refs[pieces + 2 : -4]
    tokens, units, own, arrived_sems = refs[-4:]
    copies = [
        pltpu.make_async_copy(own_ref.at[:, :, w], own.at[w], arrived_sems.at[w]) for w in range(2)
    ]
    for copy in copies:
        copy.start()
    row = 0
    for token_ref in token_refs:
        tokens[row : row + token_ref.shape[0], :] = token_ref[...]
        row += token_ref.shape[0]

    def up(weight, first):
        weight = weight.reshape(HALF, -1)
        return jnp.dot(tokens[:, first : first + HALF], weight, preferred_element_type=F32)

    def down(weight, first):
        feed = lax.dot_general(
            weight.reshape(HALF, -1),
            units[...],
            (((1,), (1,)), ((), ())),
            preferred_element_type=F32,
        ).astype(BF)
        for n, out_ref in enumerate(out_refs):
            out_ref[first : first + HALF, :] = feed[:, SHARE * n : SHARE * (n + 1)]

    sums = up(other_ref[:, :, 0], HALF)
    copies[0].wait()
    sums = sums + up(own[0], 0)
    units[...] = jax.nn.gelu(sums, approximate=True).astype(BF)
    down(other_ref[:, :, 1], HALF)
    copies[1].wait()
    down(own[1], 0)


def unit_terms(tokens, own, other):
    chunks = sum(t.shape[0] for t in tokens) // SHARE
    hidden_units = own.shape[4]
    return pl.pallas_call(
        functools.partial(units_kernel, len(tokens)),
        out_shape=[jax.ShapeDtypeStruct((ROWS, SHARE), BF)] * chunks,
        in_specs=[VMEM] * len(tokens) + [pl.BlockSpec(memory_space=pltpu.HBM), VMEM],
        out_specs=[VMEM] * chunks,
        scratch_shapes=[
            pltpu.VMEM((SHARE * chunks, ROWS), BF),
            pltpu.VMEM((SHARE * chunks, hidden_units), BF),
            pltpu.VMEM((2, 8, 2, PADDED, hidden_units), BF),
            pltpu.SemaphoreType.DMA((2,)),
        ],
        compiler_params=pltpu.CompilerParams(vmem_limit_bytes=50 << 20),
        cost_estimate=cost(4 * SHARE * chunks * ROWS * hidden_units, 4 * ROWS * hidden_units),
    )(*tokens, own, other)


def block(
    latents, queries, keys, values, log_decay, block_ids, t_index, w_mod, w_out, w_up, w_down
):
    y, c, xl = lax.axis_index("y"), lax.axis_index("c"), lax.axis_index("xl")
    place = jnp.stack([c, xl, y]).astype(jnp.int32)

    def core_half(both):
        return jnp.where(c == 0, both[..., 0, :, :], both[..., 1, :, :])

    out_mine = padded_pieces(w_out.T).reshape(2 * PADDED, -1)
    out_own = lax.all_gather(out_mine, "z", axis=0)
    out_weights = [out_own, in_vmem(along_x(out_own[:4], 1)), in_vmem(along_x(out_own[4:], -1))]
    mine = core_half(jnp.stack([padded_pieces(w_up), padded_pieces(w_down.T)]))
    queries, keys, values = queries.T, keys.T, values.T
    cumulative, packed = own_state(keys, values, log_decay)
    slices = lax.all_to_all(packed.reshape(16, -1, SHARE), ("xl", "z"), 0, 0)
    mine, _ = lax.optimization_barrier((mine, slices))
    mine_x = along_x(mine, 1)
    ahead = scan_blocks(slices)
    before = lax.all_to_all(ahead, ("xl", "z"), 0, 0).reshape(STATE_ROWS, SHARE)
    mine, mine_x, _ = lax.optimization_barrier((mine, mine_x, before))
    half = lax.all_gather(jnp.stack([mine, mine_x]), "z", axis=0)
    inner = inner_part(queries, keys, values, cumulative, block_ids[None, :])
    mixed = mix(queries, inner, cumulative, before)

    early = head_terms((2, 1), place, mixed, out_weights)
    terms = []
    for d, part in zip((2, 1), early):
        terms.append(along_y(part, d))
    mixed, _ = lax.optimization_barrier((mixed, early[0]))
    later = head_terms((3, 0), place, mixed, out_weights)
    terms += [along_y(later[0], 3), later[1]]

    shifts, step_size = modulation_of(t_index, w_mod)
    vectors = padded_pieces(shifts.reshape(4, WIDTH).T)
    latent_pieces = padded_pieces(latents.T)
    hidden, normed = norm(place, terms, in_vmem(latent_pieces), in_vmem(vectors))

    above, below = along_y(normed, -1), along_y(normed, 1)
    far = [along_y(above[: SHARE // 2], -1), along_y(below[SHARE // 2 :], 1)]
    half, _ = lax.optimization_barrier((half, normed))
    weights = [half, in_vmem(other_core(half))]
    near = unit_terms([in_vmem(above), in_vmem(below)], *weights)
    feeds = []
    for d, part in zip((1, 3), near):
        feeds.append(along_y(part, d))
    normed, _ = lax.optimization_barrier((normed, near[0]))
    rest = unit_terms([normed] + [in_vmem(f) for f in far], *weights)
    feeds += [along_y(rest[1], 2), rest[0]]
    step = step_size[None] if step_size.ndim == 0 else step_size
    velocity, advanced = last(place, step, feeds, hidden, latent_pieces, vectors)
    return (velocity.T, advanced.T)


def solution(mesh):
    fine = Mesh(mesh.devices.reshape(tuple(AXES.values())), tuple(AXES))
    pool, frame = ("xh", "c"), ("xl", "z")
    rows = P(pool + frame + ("y",), None)
    return jax.shard_map(
        block,
        mesh=fine,
        in_specs=(
            rows,
            P(pool + frame, "y"),
            P(pool + frame, "y"),
            P(pool + frame, "y"),
            P("y", pool + frame),
            P(pool + frame),
            P(pool),
            P(),
            P("y", frame),
            P(frame, "y"),
            P("y", frame),
        ),
        out_specs=(rows, rows),
        check_vma=False,
    )
```

```python
import functools
import math

import jax
import jax.numpy as jnp
import numpy as np
from jax import lax
from jax.experimental import pallas as pl
from jax.experimental.pallas import tpu as pltpu
from jax.sharding import Mesh, PartitionSpec as P


STEPS = 50
BF = jnp.bfloat16
F32 = jnp.float32
AXES = {"xh": 2, "c": 2, "xl": 2, "z": 8, "y": 4}
HEADS = 5
DH = 112
TOKENS = 512
SHARE = 128
WIDTH = 2240
PIECE = 70
PADDED = 72
PIECES = 32
ROWS = PIECES * PADDED
VMEM = pl.BlockSpec(memory_space=pltpu.VMEM)
SMEM = pl.BlockSpec(memory_space=pltpu.SMEM)
SMALL = pltpu.CompilerParams(vmem_limit_bytes=56 << 20)


def permute(block, axes, route):
    sizes = [AXES[a] for a in axes]
    pairs = []
    for i in range(int(np.prod(sizes))):
        target = route(*[int(v) for v in np.unravel_index(i, sizes)])
        if target is not None:
            pairs.append((i, int(np.ravel_multi_index(target, sizes))))
    return lax.ppermute(block, tuple(axes) if len(axes) > 1 else axes[0], pairs)


def along_y(block, d):
    return permute(block, ("y",), lambda y: ((y + d) % 4,))


def along_x(block, d):
    def route(xh, xl):
        x = (2 * xh + xl + d) % 4
        return (x // 2, x % 2)

    return permute(block, ("xh", "xl"), route)


def other_core(block):
    return permute(block, ("c",), lambda c: (1 - c,))


def in_vmem(block):
    return pltpu.with_memory_space_constraint(block, pltpu.VMEM)


def cost(flops, size):
    return pl.CostEstimate(flops=flops, bytes_accessed=size, transcendentals=0)


def modulation_of(t_index, w_mod):
    fraction = 1.0 - t_index[0].astype(F32) / STEPS
    following = fraction - 1.0 / STEPS
    sigma_now = 3.0 * fraction / (1.0 + 2.0 * fraction)
    sigma_next = 3.0 * following / (1.0 + 2.0 * following)
    half_width = w_mod.shape[0] // 2
    frequency = jnp.exp(-math.log(10000.0) * jnp.arange(half_width).astype(F32) / half_width)
    angles = 1000.0 * sigma_now * frequency
    embedding = jnp.concatenate([jnp.cos(angles), jnp.sin(angles)])
    time_features = jax.nn.silu(embedding).astype(BF)
    shifts = jnp.dot(time_features[None, :], w_mod, preferred_element_type=F32)[0]
    return (lax.optimization_barrier(shifts), sigma_next - sigma_now)


def padded_pieces(rows):
    pieces = rows.reshape(-1, PIECE, rows.shape[1])
    return jnp.pad(pieces, ((0, 0), (0, PADDED - PIECE), (0, 0)))


STATE_ROWS = 640


def total_lanes(total):
    hi = total.astype(BF).astype(F32)
    mid = (total - hi).astype(BF).astype(F32)
    low = total - hi - mid
    lane = lax.broadcasted_iota(jnp.int32, (DH, 16), 1)
    zero = jnp.zeros((DH, 16), F32)
    return jnp.where(lane == 0, hi, jnp.where(lane == 1, mid, jnp.where(lane == 2, low, zero))).astype(BF)


def state_kernel(k_ref, v_ref, decay_ref, cumulative_ref, packed_ref):
    decay = decay_ref[...]
    hi = decay.astype(BF)
    rest = decay - hi.astype(F32)
    mid = rest.astype(BF)
    low = (rest - mid.astype(F32)).astype(BF)
    row = lax.broadcasted_iota(jnp.int32, (TOKENS, TOKENS), 0)
    column = lax.broadcasted_iota(jnp.int32, (TOKENS, TOKENS), 1)
    triangle = jnp.where(row <= column, 1.0, 0.0).astype(BF)
    cumulative = sum(
        jnp.dot(part, triangle, preferred_element_type=F32) for part in (low, mid, hi)
    )
    cumulative_ref[...] = cumulative
    for h in range(HEADS):
        mine = cumulative[h : h + 1, :]
        total = mine[:, TOKENS - 1 :]
        heads = pl.ds(DH * h, DH)
        scaled = (k_ref[heads, :].astype(F32) * jnp.exp(total - mine)).astype(BF)
        state = lax.dot_general(
            v_ref[heads, :], scaled, (((1,), (1,)), ((), ())), preferred_element_type=F32
        )
        packed_ref[heads, 0:DH] = state.astype(BF)
        packed_ref[heads, DH:SHARE] = total_lanes(total)
    packed_ref[HEADS * DH :, :] = jnp.zeros((STATE_ROWS - HEADS * DH, SHARE), BF)


def own_state(keys, values, log_decay):
    return pl.pallas_call(
        state_kernel,
        out_shape=(
            jax.ShapeDtypeStruct((HEADS, TOKENS), F32),
            jax.ShapeDtypeStruct((STATE_ROWS, SHARE), BF),
        ),
        in_specs=[VMEM] * 3,
        out_specs=(VMEM, VMEM),
        cost_estimate=cost(10**9, 3 * 10**6),
    )(keys, values, log_decay)


def scan_kernel(blocks_ref, before_ref):
    state = jnp.zeros(before_ref.shape[1:], F32)
    for f in range(blocks_ref.shape[0]):
        before_ref[f] = state.astype(BF)
        packed = blocks_ref[f].astype(F32)
        total = jnp.sum(packed[:, DH : DH + 3], axis=1, keepdims=True)
        state = packed + jnp.exp(total) * state


def scan_blocks(blocks):
    return pl.pallas_call(
        scan_kernel,
        out_shape=jax.ShapeDtypeStruct(blocks.shape, BF),
        in_specs=[VMEM],
        out_specs=VMEM,
        cost_estimate=cost(10**6, 10**6),
    )(in_vmem(blocks))


def inner_kernel(q_ref, k_ref, v_ref, cumulative_ref, labels_ref, out_ref):
    cumulative = cumulative_ref[...]
    labels = labels_ref[...].astype(F32)
    stacked = jnp.concatenate([cumulative, labels, jnp.zeros((2, TOKENS), F32)], axis=0)
    columns = stacked.T
    visible = columns[:, HEADS : HEADS + 1] <= labels
    for h in range(HEADS):
        heads = pl.ds(DH * h, DH)
        scores = lax.dot_general(
            k_ref[heads, :], q_ref[heads, :], (((0,), (0,)), ((), ())), preferred_element_type=F32
        )
        decay = jnp.exp(jnp.minimum(cumulative[h : h + 1, :] - columns[:, h : h + 1], 0.0))
        weights = jnp.where(visible, decay * (DH**-0.5), 0.0)
        probs = (scores * weights).astype(BF)
        out_ref[heads, :] = jnp.dot(v_ref[heads, :], probs, preferred_element_type=F32)


def inner_part(queries, keys, values, cumulative, labels):
    return pl.pallas_call(
        inner_kernel,
        out_shape=jax.ShapeDtypeStruct((HEADS * DH, TOKENS), F32),
        in_specs=[VMEM] * 5,
        out_specs=VMEM,
        cost_estimate=cost(5 * 10**9, 4 * 10**6),
    )(queries, keys, values, cumulative, labels)


def mix_kernel(q_ref, inner_ref, cumulative_ref, before_ref, out_ref):
    for h in range(HEADS):
        heads = pl.ds(DH * h, DH)
        carried = jnp.dot(
            before_ref[heads, :][:, 0:DH], q_ref[heads, :], preferred_element_type=F32
        )
        numerator = inner_ref[heads, :] + carried * (
            jnp.exp(cumulative_ref[h : h + 1, :]) * (DH**-0.5)
        )
        mean = jnp.sum(numerator * numerator, axis=0, keepdims=True) * (1.0 / DH)
        out_ref[heads, :] = (numerator * lax.rsqrt(mean + 1e-06)).astype(BF)


def mix(queries, inner, cumulative, before):
    return pl.pallas_call(
        mix_kernel,
        out_shape=jax.ShapeDtypeStruct((HEADS * DH, TOKENS), BF),
        in_specs=[VMEM] * 4,
        out_specs=VMEM,
        cost_estimate=cost(10**8, 4 * 10**6),
    )(queries, inner, cumulative, in_vmem(before))


def head_kernel(distances, place_ref, mixed_ref, own_ref, first_ref, second_ref, *out_refs):
    for d, out_ref in zip(distances, out_refs):
        start = pl.multiple_of(((place_ref[2] + d) % 4) * SHARE, SHARE)
        tokens = mixed_ref[:, pl.ds(start, SHARE)]
        row = 0
        for weight_ref in (own_ref, first_ref, second_ref):
            weight = weight_ref[...].reshape(-1, weight_ref.shape[2])
            rows = weight.shape[0]
            out_ref[row : row + rows, :] = jnp.dot(
                weight, tokens, preferred_element_type=F32
            ).astype(BF)
            row += rows


def head_terms(distances, place, mixed, weights):
    return pl.pallas_call(
        functools.partial(head_kernel, distances),
        out_shape=[jax.ShapeDtypeStruct((ROWS, SHARE), BF)] * len(distances),
        in_specs=[SMEM] + [VMEM] * 4,
        out_specs=[VMEM] * len(distances),
        cost_estimate=cost(10**9, 4 * 10**6),
        compiler_params=SMALL,
    )(place, mixed, *weights)


def piece_table(place_ref):
    c, xl = place_ref[0], place_ref[1]
    for hr in range(2):
        for z in range(8):
            for xr in range(2):
                h = c if hr == 0 else 1 - c
                x = xl if xr == 0 else 1 - xl
                yield hr * 16 + z * 2 + xr, 2 * (8 * x + z) + h, 16 * xr + 2 * z + h


def norm_kernel(place_ref, t0, t1, t2, t3, latent_ref, vector_ref, hidden_ref, normed_ref, work):
    sums = jnp.zeros((PADDED, SHARE), F32)
    for own, natural, term in piece_table(place_ref):
        attention = sum(t[term].astype(F32) for t in (t0, t1, t2, t3))
        hidden = latent_ref[natural].astype(F32) + vector_ref[natural][:, 3:4] * attention
        hidden_ref[own] = hidden
        sums = sums + hidden
    mean = jnp.sum(sums, axis=0, keepdims=True) * (1.0 / WIDTH)
    real = lax.broadcasted_iota(jnp.int32, (PADDED, SHARE), 0) < PIECE
    squares = jnp.zeros((PADDED, SHARE), F32)
    for own in range(PIECES):
        centered = hidden_ref[own] - mean
        squares = squares + centered * centered
    squares = jnp.where(real, squares, 0.0)
    scaling = lax.rsqrt(jnp.sum(squares, axis=0, keepdims=True) * (1.0 / WIDTH) + 1e-06)
    for own, natural, _ in piece_table(place_ref):
        vectors = vector_ref[natural]
        normed = (hidden_ref[own] - mean) * scaling * (1.0 + vectors[:, 1:2]) + vectors[:, 0:1]
        work[own * PADDED : (own + 1) * PADDED, :] = jnp.where(real, normed, 0.0)
    for i in range(ROWS // 256):
        normed_ref[:, 256 * i : 256 * (i + 1)] = work[256 * i : 256 * (i + 1), :].T.astype(BF)


def arrived(parts):
    pieces = [p.reshape(PIECES, PADDED, SHARE) for p in parts]
    return [in_vmem(p) for p in pieces[:-1]] + pieces[-1:]


def norm(place, terms, latents, vectors):
    return pl.pallas_call(
        norm_kernel,
        out_shape=(
            jax.ShapeDtypeStruct((PIECES, PADDED, SHARE), F32),
            jax.ShapeDtypeStruct((SHARE, ROWS), BF),
        ),
        in_specs=[SMEM] + [VMEM] * 6,
        out_specs=(VMEM, VMEM),
        scratch_shapes=[pltpu.VMEM((ROWS, SHARE), F32)],
        cost_estimate=cost(10**7, 8 * 10**6),
        compiler_params=SMALL,
    )(place, *arrived(terms), latents, vectors)


def last_kernel(place_ref, step_ref, f0, f1, f2, f3, hidden_ref, latent_ref, vector_ref, v_ref, a_ref, v_work, a_work):
    step = step_ref[0]
    c, xl = place_ref[0], place_ref[1]
    for natural in range(PIECES):
        f, h = natural // 2, natural % 2
        hr = c if h == 0 else 1 - c
        xr = xl if f < 8 else 1 - xl
        own = hr * 16 + (f % 8) * 2 + xr
        feed = sum(f[own].astype(F32) for f in (f0, f1, f2, f3))
        velocity = (hidden_ref[own] + vector_ref[natural][:, 2:3] * feed).astype(BF).astype(F32)
        rows = slice(PIECE * natural, PIECE * (natural + 1))
        v_work[rows, :] = velocity[:PIECE]
        a_work[rows, :] = (latent_ref[natural].astype(F32) + step * velocity)[:PIECE]
    v_ref[...] = v_work[...].astype(BF)
    a_ref[...] = a_work[...].astype(BF)


def last(place, step_size, feeds, hidden, latents, vectors):
    shape = jax.ShapeDtypeStruct((WIDTH, SHARE), BF)
    return pl.pallas_call(
        last_kernel,
        out_shape=(shape, shape),
        in_specs=[SMEM] * 2 + [VMEM] * 7,
        out_specs=(VMEM, VMEM),
        scratch_shapes=[pltpu.VMEM((WIDTH, SHARE), F32)] * 2,
        cost_estimate=cost(10**7, 8 * 10**6),
        compiler_params=SMALL,
    )(place, step_size, *arrived(feeds), hidden, latents, vectors)


HALF = ROWS // 2


def stacked(token_refs, tokens):
    row = 0
    for token_ref in token_refs:
        tokens[row : row + token_ref.shape[0], :] = token_ref[...]
        row += token_ref.shape[0]


def up_kernel(pieces, *refs):
    own_ref, out_ref, tokens = refs[pieces:]
    stacked(refs[:pieces], tokens)
    weight = own_ref[...].reshape(HALF, -1)
    out_ref[...] = jnp.dot(tokens[:, 0:HALF], weight, preferred_element_type=F32)


def own_sums(tokens, own):
    rows = sum(t.shape[0] for t in tokens)
    hidden_units = own.shape[4]
    block = (8, 2, 1, PADDED, hidden_units)
    return pl.pallas_call(
        functools.partial(up_kernel, len(tokens)),
        grid=(1,),
        out_shape=jax.ShapeDtypeStruct((rows, hidden_units), F32),
        in_specs=[pl.BlockSpec(t.shape, lambda i: (0, 0)) for t in tokens]
        + [pl.BlockSpec(block, lambda i: (0, 0, 0, 0, 0))],
        out_specs=pl.BlockSpec((rows, hidden_units), lambda i: (0, 0)),
        scratch_shapes=[pltpu.VMEM((rows, ROWS), BF)],
        cost_estimate=cost(rows * ROWS * hidden_units, ROWS * hidden_units),
        compiler_params=SMALL,
    )(*tokens, own)


def units_kernel(pieces, with_sums, *refs):
    own_ref, other_ref = refs[pieces : pieces + 2]
    out_refs = refs[pieces + 2 + with_sums : -4]
    tokens, units, own, arrived_sems = refs[-4:]
    copies = [
        pltpu.make_async_copy(own_ref.at[:, :, w], own.at[w], arrived_sems.at[w]) for w in range(2)
    ]
    for copy in copies[with_sums:]:
        copy.start()
    stacked(refs[:pieces], tokens)

    def up(weight, first):
        weight = weight.reshape(HALF, -1)
        return jnp.dot(tokens[:, first : first + HALF], weight, preferred_element_type=F32)

    def down(weight, first):
        feed = lax.dot_general(
            weight.reshape(HALF, -1),
            units[...],
            (((1,), (1,)), ((), ())),
            preferred_element_type=F32,
        ).astype(BF)
        for n, out_ref in enumerate(out_refs):
            out_ref[first : first + HALF, :] = feed[:, SHARE * n : SHARE * (n + 1)]

    sums = up(other_ref[:, :, 0], HALF)
    if with_sums:
        sums = sums + refs[pieces + 2][...]
    else:
        copies[0].wait()
        sums = sums + up(own[0], 0)
    units[...] = jax.nn.gelu(sums, approximate=True).astype(BF)
    down(other_ref[:, :, 1], HALF)
    copies[1].wait()
    down(own[1], 0)


def unit_terms(tokens, own, other, sums=()):
    chunks = sum(t.shape[0] for t in tokens) // SHARE
    hidden_units = own.shape[4]
    return pl.pallas_call(
        functools.partial(units_kernel, len(tokens), len(sums)),
        out_shape=[jax.ShapeDtypeStruct((ROWS, SHARE), BF)] * chunks,
        in_specs=[VMEM] * len(tokens)
        + [pl.BlockSpec(memory_space=pltpu.HBM), VMEM]
        + [VMEM] * len(sums),
        out_specs=[VMEM] * chunks,
        scratch_shapes=[
            pltpu.VMEM((SHARE * chunks, ROWS), BF),
            pltpu.VMEM((SHARE * chunks, hidden_units), BF),
            pltpu.VMEM((2, 8, 2, PADDED, hidden_units), BF),
            pltpu.SemaphoreType.DMA((2,)),
        ],
        compiler_params=pltpu.CompilerParams(vmem_limit_bytes=48 << 20),
        cost_estimate=cost(4 * SHARE * chunks * ROWS * hidden_units, 4 * ROWS * hidden_units),
    )(*tokens, own, other, *sums)


def block(
    latents, queries, keys, values, log_decay, block_ids, t_index, w_mod, w_out, w_up, w_down
):
    y, c, xl = lax.axis_index("y"), lax.axis_index("c"), lax.axis_index("xl")
    place = jnp.stack([c, xl, y]).astype(jnp.int32)

    def core_half(both):
        return jnp.where(c == 0, both[..., 0, :, :], both[..., 1, :, :])

    out_mine = padded_pieces(w_out.T).reshape(2 * PADDED, -1)
    out_own = lax.all_gather(out_mine, "z", axis=0)
    out_weights = [out_own, in_vmem(along_x(out_own[:4], 1)), in_vmem(along_x(out_own[4:], -1))]
    mine = core_half(jnp.stack([padded_pieces(w_up), padded_pieces(w_down.T)]))
    queries, keys, values = queries.T, keys.T, values.T
    cumulative, packed = own_state(keys, values, log_decay)
    slices = lax.all_to_all(packed.reshape(16, -1, SHARE), ("xl", "z"), 0, 0)
    mine, _ = lax.optimization_barrier((mine, slices))
    mine_x = along_x(mine, 1)
    ahead = scan_blocks(slices)
    before = lax.all_to_all(ahead, ("xl", "z"), 0, 0).reshape(STATE_ROWS, SHARE)
    mine, mine_x, _ = lax.optimization_barrier((mine, mine_x, before))
    half = lax.all_gather(jnp.stack([mine, mine_x]), "z", axis=0)
    inner = inner_part(queries, keys, values, cumulative, block_ids[None, :])
    mixed = mix(queries, inner, cumulative, before)

    early = head_terms((2, 1), place, mixed, out_weights)
    terms = []
    for d, part in zip((2, 1), early):
        terms.append(along_y(part, d))
    mixed, _ = lax.optimization_barrier((mixed, early[0]))
    later = head_terms((3, 0), place, mixed, out_weights)
    terms += [along_y(later[0], 3), later[1]]

    shifts, step_size = modulation_of(t_index, w_mod)
    vectors = padded_pieces(shifts.reshape(4, WIDTH).T)
    latent_pieces = padded_pieces(latents.T)
    hidden, normed = norm(place, terms, in_vmem(latent_pieces), in_vmem(vectors))

    above, below = along_y(normed, -1), along_y(normed, 1)
    far = [along_y(above[: SHARE // 2], -1), along_y(below[SHARE // 2 :], 1)]
    half, _ = lax.optimization_barrier((half, normed))
    weights = [half, in_vmem(other_core(half))]
    sums = own_sums([above, below], half)
    near = unit_terms([above, below], *weights, [sums])
    feeds = []
    for d, part in zip((1, 3), near):
        feeds.append(along_y(part, d))
    normed, _ = lax.optimization_barrier((normed, near[0]))
    rest = unit_terms([normed] + [in_vmem(f) for f in far], *weights)
    feeds += [along_y(rest[1], 2), rest[0]]
    step = step_size[None] if step_size.ndim == 0 else step_size
    velocity, advanced = last(place, step, feeds, hidden, latent_pieces, vectors)
    return (velocity.T, advanced.T)


def solution(mesh):
    fine = Mesh(mesh.devices.reshape(tuple(AXES.values())), tuple(AXES))
    pool, frame = ("xh", "c"), ("xl", "z")
    rows = P(pool + frame + ("y",), None)
    return jax.shard_map(
        block,
        mesh=fine,
        in_specs=(
            rows,
            P(pool + frame, "y"),
            P(pool + frame, "y"),
            P(pool + frame, "y"),
            P("y", pool + frame),
            P(pool + frame),
            P(pool),
            P(),
            P("y", frame),
            P(frame, "y"),
            P("y", frame),
        ),
        out_specs=(rows, rows),
        check_vma=False,
    )
```
